256 devices in a mesh: tx: 4 (over x), ty: 8 (over y, core), pos: 8 (over z).
Axes of the slice: x: 4, y: 4, z: 8, core: 2. Of those that a mesh axis runs over, the one named last changes fastest.
Arguments:
- obj: float32 [2, 3072, 6144], P(None, 'tx', 'ty'), may hold values from -5 to 5
- probe: float32 [4, 2, 128, 128], replicated, may hold values from -6 to 6
- measured: bfloat16 [4096, 128, 128], P(('tx', 'ty', 'pos')), may hold values from 0 to 4
- tile_of: int32 [4096, 1], replicated, may hold values from 0 to 31; in each aligned block of 16 rows (0 to 15, 16 to 31, ...) at most 2 rows name the same one
- inner: int32 [4096, 2], replicated, may hold values from 0 to 640
Outputs:
- obj_grad: float32 [2, 3072, 6144], P(None, ('tx', 'pos'), 'ty')
- probe_grad: float32 [4, 2, 128, 128], replicated
- misfit: float32 [4096], P(('tx', 'ty', 'pos'))
The draws below stay inside these ranges and needn't reach their ends.
Inputs may be any that keep to these rules, and one draw needn't show every extreme that they name: `tile_of`: tile number: tile row index times the number of tile columns plus tile column index; among the 16 positions of one device no tile is named more than 2 times.
All inputs are finite; a program needn't handle non-finite values.
Results may differ from the reference program's by a relative error of at most 0.00075.
The reference program's roundings to bfloat16 on the way count: a program that leaves them out, or rounds other values in their place, can miss the bound.
Values may be sent and summed in bfloat16 or wider, within the bound.
No kernel may reach another device: no remote copies, remote signals or barrier semaphores. Data moves between devices by JAX's collectives and lax.ppermute only.
A program may use at most 128 MiB of HBM per device.

```python
import math
import jax
import jax.numpy as jnp
import numpy as np
from jax import lax

M = 128
MODES = 4
DEVICE_POSITIONS = 16
TILE = 768
CAP = 2
P_SIZE = 4096
NR = 3072
NC = 6144
N_TX = 4
N_TY = 8


def set_ends(array, key, low, high):
    dims = array.shape
    index_at = [jax.random.randint(jax.random.fold_in(key, axis), (), 0, dims[axis]) for axis in range(len(dims))]
    array = array.at[tuple(index_at)].set(low)
    longest = dims.index(max(dims))
    index_at[longest] = (index_at[longest] + 1) % dims[longest]
    return array.at[tuple(index_at)].set(high)


def steps_of(own_key, extent, pieces, low, high):
    factor_of, own = 1.0, jax.random.fold_in(own_key, 6)
    for position, blocks in pieces:
        heights = jnp.exp(jax.random.uniform(jax.random.fold_in(own, position), (blocks,), jnp.float32, low / len(pieces), high / len(pieces)))
        factor_of = factor_of * jnp.repeat(heights, extent[position] // blocks).reshape([-1 if axis == position else 1 for axis in range(len(extent))])
    return factor_of


def routed_block(stream_key, own, number, rows, count, top, most, slope):
    order = jax.random.permutation(stream_key, count)
    heavy_load, usual = portions_of(count, rows * top, most, slope, True), portions_of(count, rows * top, most, slope, False)
    places = jnp.arange(count)

    def named(lengths, rotation):
        used = int((lengths > 0).sum())
        fixed = max(1, used // 4)
        moved = fixed + (places - fixed + rotation * (used - fixed)) % max(1, count - fixed)
        return jnp.zeros((count,), jnp.int32).at[order[jnp.where(places < fixed, places, moved)]].set(jnp.asarray(lengths, jnp.int32))

    lengths = jnp.where(number % 4 == 0, named(heavy_load, number // 4), named(usual, number - number // 4 - 1))
    mixed = jax.random.permutation(jax.random.fold_in(own, 3), count)
    source_of, sink = mixed[0:count // 2 * 2:2], mixed[1:count // 2 * 2:2]
    room = jnp.minimum(lengths[source_of] - 1, most - lengths[sink]) // 2
    room = jnp.where((source_of == order[0]) | (sink == order[0]) | (lengths[sink] == 0), 0, jnp.maximum(room, 0))
    moved = jax.random.randint(jax.random.fold_in(own, 4), (count // 2,), 0, 1 << 20) % (room + 1)
    lengths = lengths.at[source_of].add(-moved).at[sink].add(moved)
    items = jnp.searchsorted(jnp.cumsum(lengths), jnp.arange(rows * top), side="right").astype(jnp.int32)
    grid = items.reshape(top, rows).T
    grid = grid[jax.random.permutation(jax.random.fold_in(own, 1), rows)]
    rotation = jax.random.randint(jax.random.fold_in(own, 2), (rows, 1), 0, top)
    return jnp.take_along_axis(grid, (jnp.arange(top)[None, :] + rotation) % top, axis=1)


def portions_of(amount, total, limit, lean, full):
    loads = [(1 << 20) // math.isqrt(rank ** lean) + 1 for rank in range(1, amount + 1)]
    largest = limit if full else min(limit, max(-(-total // amount), total * loads[0] // sum(loads)))
    least = 1 if total - largest >= amount - 1 else 0
    counts, spare = [largest] + [least] * (amount - 1), total - largest - least * (amount - 1)
    while spare > 0:
        free = [i for i in range(1, amount) if counts[i] < largest] or [i for i in range(1, amount) if counts[i] < limit]
        pool, left = sum([loads[i] for i in free]), spare
        for i in free:
            addition = min(limit - counts[i], max(1, left * loads[i] // pool), spare)
            counts[i] = counts[i] + addition
            spare = spare - addition
    return np.array(counts)


def scatter_about(rng, dims, spread, bound, cuts=(), kind=jnp.bfloat16):
    entries = spread * jax.random.normal(rng, dims, jnp.float32)
    if cuts:
        entries = entries * steps_of(rng, dims, cuts, -0.22, 0.18)
    return jnp.clip(entries, -bound, bound).astype(kind)


def setup_inputs(seed: int = 0) -> dict:
    streams_of = jax.random.split(jax.random.key(seed), 6)
    obj = scatter_about(streams_of[0], (2, NR, NC), 0.7, 5.0, ((1, 4), (2, 8)), jnp.float32)
    probe = scatter_about(streams_of[1], (MODES, 2, M, M), 1.0, 6.0, (), jnp.float32)
    measured = jnp.clip(4.0 * jax.random.uniform(streams_of[2], (P_SIZE, M, M), jnp.float32) ** steps_of(streams_of[2], (P_SIZE, M, M), ((0, 256),), -0.2, 0.2), 0.0, 4.0).astype(jnp.bfloat16)
    tile_of_keys = jax.random.split(jax.random.fold_in(streams_of[3], 1), P_SIZE // DEVICE_POSITIONS)
    tile_of_turns = jax.random.permutation(jax.random.fold_in(streams_of[3], 3), P_SIZE // DEVICE_POSITIONS)
    tile_of = jax.vmap(lambda own, number: routed_block(jax.random.fold_in(streams_of[3], 2), own, number, DEVICE_POSITIONS, N_TX * N_TY, 1, CAP, 2))(tile_of_keys, tile_of_turns).reshape((P_SIZE, 1))
    inner = set_ends(jax.random.randint(streams_of[4], (P_SIZE, 2), 0, TILE - M + 1), jax.random.fold_in(streams_of[4], 1), 0, TILE - M).astype(jnp.int32)
    return {"obj": obj, "probe": probe, "measured": measured, "tile_of": tile_of, "inner": inner}


def dft_tables(width):
    counter = jnp.arange(width, dtype=jnp.int32)
    product = counter[:, None] * counter[None, :] % width
    angles = product.astype(jnp.float32) * (2.0 * jnp.pi / width)
    factor = 1.0 / jnp.sqrt(jnp.float32(width))
    return ((jnp.cos(angles) * factor).astype(jnp.bfloat16), (-jnp.sin(angles) * factor).astype(jnp.bfloat16))

def right_product(field, table):
    return jnp.einsum('...jk,kl->...jl', field.astype(jnp.float32), table.astype(jnp.float32), precision=lax.Precision.HIGHEST)

def left_product(table, field):
    return jnp.einsum('ij,...jl->...il', table.astype(jnp.float32), field.astype(jnp.float32), precision=lax.Precision.HIGHEST)

def transform(real_part, imag_part, table_real_values, table_imaginary):
    half_real = (right_product(real_part, table_real_values) - right_product(imag_part, table_imaginary)).astype(jnp.bfloat16)
    half_imag = (right_product(real_part, table_imaginary) + right_product(imag_part, table_real_values)).astype(jnp.bfloat16)
    whole_real = left_product(table_real_values, half_real) - left_product(table_imaginary, half_imag)
    whole_imag = left_product(table_real_values, half_imag) + left_product(table_imaginary, half_real)
    return (whole_real, whole_imag)

def position_contributions(patch_stack, probe, measured, table_real_values, table_imaginary):
    obj_real = patch_stack[:, 0].astype(jnp.float32)[:, None]
    obj_imag = patch_stack[:, 1].astype(jnp.float32)[:, None]
    probe_real = probe[:, 0][None]
    probe_imag = probe[:, 1][None]
    wave_real = (probe_real * obj_real - probe_imag * obj_imag).astype(jnp.bfloat16)
    wave_imag = (probe_real * obj_imag + probe_imag * obj_real).astype(jnp.bfloat16)
    far_real, far_imag = transform(wave_real, wave_imag, table_real_values, table_imaginary)
    intensity = lax.optimization_barrier(jnp.sum(far_real * far_real + far_imag * far_imag, axis=1))
    model_amp = jnp.sqrt(intensity + 1.0)
    data_amp = measured.astype(jnp.float32)
    misfit = lax.optimization_barrier(jnp.mean((model_amp - data_amp) * (model_amp - data_amp), axis=(1, 2)))
    factor = (1.0 - data_amp / model_amp)[:, None]
    resid_real = (far_real * factor).astype(jnp.bfloat16)
    resid_imag = (far_imag * factor).astype(jnp.bfloat16)
    back_real, back_imag = transform(resid_real, resid_imag, table_real_values, -table_imaginary)
    object_share = jnp.stack([lax.optimization_barrier(jnp.sum(probe_real * back_real + probe_imag * back_imag, axis=1)), lax.optimization_barrier(jnp.sum(probe_real * back_imag - probe_imag * back_real, axis=1))], axis=1)
    probe_share = jnp.stack([lax.optimization_barrier(jnp.sum(obj_real * back_real + obj_imag * back_imag, axis=0)), lax.optimization_barrier(jnp.sum(obj_real * back_imag - obj_imag * back_real, axis=0))], axis=1)
    return (object_share, probe_share, misfit)

def reference(obj, probe, measured, tile_of, inner):
    table_real_values, table_imaginary = dft_tables(M)
    tiles = tile_of[:, 0].astype(jnp.int32)
    rows = (tiles // N_TY * TILE + inner[:, 0]).astype(jnp.int32)
    cols = (tiles % N_TY * TILE + inner[:, 1]).astype(jnp.int32)
    rounded = obj.astype(jnp.bfloat16)
    anchor = jnp.zeros((), jnp.int32)

    def cut(row, col):
        return lax.dynamic_slice(rounded, (anchor, row, col), (2, M, M))

    def one_block(carry, number):
        total, probe_total = carry
        first_position = (number * DEVICE_POSITIONS).astype(jnp.int32)
        block_rows = lax.dynamic_slice_in_dim(rows, first_position, DEVICE_POSITIONS)
        block_cols = lax.dynamic_slice_in_dim(cols, first_position, DEVICE_POSITIONS)
        patch_stack = jax.vmap(cut)(block_rows, block_cols)
        block_measurements = lax.dynamic_slice_in_dim(measured, first_position, DEVICE_POSITIONS, 0)
        object_share, probe_share, misfit = position_contributions(patch_stack, probe, block_measurements, table_real_values, table_imaginary)

        def add_one(item, accum):
            current = lax.dynamic_slice(accum, (anchor, block_rows[item], block_cols[item]), (2, M, M))
            return lax.dynamic_update_slice(accum, current + object_share[item], (anchor, block_rows[item], block_cols[item]))
        total = lax.fori_loop(0, DEVICE_POSITIONS, add_one, total)
        return ((total, probe_total + probe_share), misfit)
    start_state = (jnp.zeros((2, NR, NC), jnp.float32), jnp.zeros((MODES, 2, M, M), jnp.float32))
    (total, probe_total), misfits = lax.scan(one_block, start_state, jnp.arange(P_SIZE // DEVICE_POSITIONS, dtype=jnp.int32))
    return (total, probe_total / P_SIZE, misfits.reshape(P_SIZE))
```

```python
import jax
import jax.numpy as jnp
import ml_dtypes
import numpy as np
from jax import lax
from jax.experimental import pallas as pl
from jax.experimental.pallas import tpu as pltpu
from jax.sharding import PartitionSpec as P

CAP = 2
LANES = 128
ROW_BITS = 10
TILE_SHIFT = 2 * ROW_BITS
LOW = (1 << ROW_BITS) - 1


def dft_blocks(width):
    counter = np.arange(width, dtype=np.int32)
    product = counter[:, None] * counter[None, :] % width
    angles = product.astype(np.float32) * np.float32(2.0 * np.pi / width)
    factor = np.float32(1.0) / np.sqrt(np.float32(width))
    c = (np.cos(angles) * factor).astype(ml_dtypes.bfloat16)
    s = (-np.sin(angles) * factor).astype(ml_dtypes.bfloat16)
    return np.block([[c, -s], [s, c]]), np.block([[c, s], [-s, c]])


def send_kernel(groups, depth, per_device, where_ref, packed_ref, measured_ref, out_ref, slot_ref, sems):
    base = (where_ref[0] * depth + where_ref[1]) * per_device
    tiles = [lax.shift_right_logical(packed_ref[base + i], TILE_SHIFT) for i in range(per_device)]
    copies = []
    for i in range(per_device):
        rank = jnp.int32(0)
        for j in range(i):
            rank = rank + (tiles[j] == tiles[i]).astype(jnp.int32)
        slot = tiles[i] * CAP + rank
        slot_ref[i] = slot
        copy = pltpu.make_async_copy(measured_ref.at[i], out_ref.at[slot], sems.at[i])
        copy.start()
        copies.append(copy)
    for copy in copies:
        copy.wait()


def list_kernel(groups, depth, per_device, where_ref, packed_ref, list_ref):
    tile = where_ref[0]
    plane = where_ref[1]

    def one_group(group, count):
        base = (group * depth + plane) * per_device
        rank = jnp.int32(0)
        for i in range(per_device):
            value = packed_ref[base + i]
            hit = (lax.shift_right_logical(value, TILE_SHIFT) == tile).astype(jnp.int32)
            slot = group * CAP + rank
            list_ref[count] = (slot << TILE_SHIFT) | (value & ((1 << TILE_SHIFT) - 1))
            count = count + hit
            rank = rank + hit
        return count

    count = lax.fori_loop(0, groups, one_group, jnp.int32(0))
    list_ref[groups * CAP + 1] = count


def main_kernel(
    modes,
    slots,
    list_ref,
    obj_ref,
    probe_ref,
    arrived_ref,
    x_ref,
    y_ref,
    grad_ref,
    sums_ref,
    tile_s,
    acc_s,
    probe_s,
    meas_s,
    misfit_s,
    sems,
):
    width = LANES
    blocks = tile_s.shape[1]
    copies = []
    for a in range(2):
        for b in range(blocks):
            copies.append(
                pltpu.make_async_copy(
                    obj_ref.at[a, :, pl.ds(b * LANES, LANES)], tile_s.at[a, b], sems.at[a * blocks + b]
                )
            )
    copies.append(pltpu.make_async_copy(arrived_ref, meas_s, sems.at[2 * blocks]))
    for copy in copies:
        copy.start()
    acc_s[...] = jnp.zeros_like(acc_s)
    probe_s[...] = jnp.zeros_like(probe_s)
    misfit_s[...] = jnp.zeros_like(misfit_s)
    for copy in copies:
        copy.wait()
    lane = lax.broadcasted_iota(jnp.int32, (width, LANES), 1)

    def one(item, carry):
        entry = list_ref[item]
        slot = lax.shift_right_logical(entry, TILE_SHIFT)
        row = lax.shift_right_logical(entry, ROW_BITS) & LOW
        col = entry & LOW
        block = jnp.minimum(lax.shift_right_logical(col, 7), blocks - 2)
        shift = col - block * LANES
        back_shift = (LANES - shift) & (LANES - 1)
        own = lane < LANES - shift

        def cut(a):
            left = pltpu.roll(tile_s[a, block, pl.ds(row, width), :], back_shift, 1)
            right = pltpu.roll(tile_s[a, block + 1, pl.ds(row, width), :], back_shift, 1)
            return jnp.where(own, left, right).astype(jnp.bfloat16).astype(jnp.float32)

        obj_r = cut(0)
        obj_i = cut(1)
        waves = []
        for k in range(modes):
            p_r = probe_ref[k, 0]
            p_i = probe_ref[k, 1]
            waves.append(
                jnp.concatenate([p_r * obj_r - p_i * obj_i, p_r * obj_i + p_i * obj_r], axis=1).astype(
                    jnp.bfloat16
                )
            )

        def stack(half):
            return jnp.concatenate(
                [
                    jnp.concatenate(
                        [half[k * width : (k + 1) * width, :width], half[k * width : (k + 1) * width, width:]],
                        axis=0,
                    )
                    for k in range(modes)
                ],
                axis=1,
            )

        half = jnp.dot(jnp.concatenate(waves, axis=0), y_ref[...], preferred_element_type=jnp.float32)
        far = jnp.dot(x_ref[...], stack(half.astype(jnp.bfloat16)), preferred_element_type=jnp.float32)
        intensity = jnp.ones((width, LANES), jnp.float32)
        for k in range(modes):
            f_r = far[:width, k * width : (k + 1) * width]
            f_i = far[width:, k * width : (k + 1) * width]
            intensity = intensity + (f_r * f_r + f_i * f_i)
        data = meas_s[slot].astype(jnp.float32)
        inverse = lax.rsqrt(intensity)
        gap = intensity * inverse - data
        misfit_s[slot] = jnp.sum(gap * gap, axis=0, keepdims=True)
        factor = 1.0 - data * inverse
        residuals = []
        for k in range(modes):
            f_r = far[:width, k * width : (k + 1) * width]
            f_i = far[width:, k * width : (k + 1) * width]
            residuals.append(jnp.concatenate([f_r * factor, f_i * factor], axis=1).astype(jnp.bfloat16))
        half = jnp.dot(jnp.concatenate(residuals, axis=0), x_ref[...], preferred_element_type=jnp.float32)
        back = jnp.dot(y_ref[...], stack(half.astype(jnp.bfloat16)), preferred_element_type=jnp.float32)
        part_r = jnp.zeros((width, LANES), jnp.float32)
        part_i = jnp.zeros((width, LANES), jnp.float32)
        for k in range(modes):
            p_r = probe_ref[k, 0]
            p_i = probe_ref[k, 1]
            b_r = back[:width, k * width : (k + 1) * width]
            b_i = back[width:, k * width : (k + 1) * width]
            part_r = part_r + (p_r * b_r + p_i * b_i)
            part_i = part_i + (p_r * b_i - p_i * b_r)
            probe_s[k, 0] = probe_s[k, 0] + (obj_r * b_r + obj_i * b_i)
            probe_s[k, 1] = probe_s[k, 1] + (obj_r * b_i - obj_i * b_r)
        keep = lane >= shift
        for a, part in ((0, part_r), (1, part_i)):
            turned = pltpu.roll(part, shift & (LANES - 1), 1)
            spot = (a, block, pl.ds(row, width), slice(None))
            acc_s[spot] = acc_s[spot] + jnp.where(keep, turned, 0.0)
            spot = (a, block + 1, pl.ds(row, width), slice(None))
            acc_s[spot] = acc_s[spot] + jnp.where(keep, 0.0, turned)
        return carry

    lax.fori_loop(0, list_ref[slots + 1], one, jnp.int32(0))
    groups = sums_ref.shape[0]
    rows = sums_ref.shape[1] - 8
    copies = []
    for a in range(2):
        for b in range(blocks):
            copies.append(
                pltpu.make_async_copy(
                    acc_s.at[a, b], grad_ref.at[a, :, pl.ds(b * LANES, LANES)], sems.at[a * blocks + b]
                )
            )
    for copy in copies:
        copy.start()
    flat = modes * 2 * width // groups
    per_plane = width // flat
    for g in range(groups):
        plane, part = divmod(g, per_plane)
        sums_ref[g, pl.ds(0, rows), :] = probe_s[plane // 2, plane % 2, pl.ds(part * flat, flat), :]
        for s in range(CAP):
            sums_ref[g, pl.ds(rows + s, 1), :] = misfit_s[g * CAP + s]
        sums_ref[g, pl.ds(rows + CAP, 8 - CAP), :] = jnp.zeros((8 - CAP, LANES), jnp.float32)
    for copy in copies:
        copy.wait()


def receive_kernel(scale, pixels, slot_ref, sums_ref, probe_ref, misfit_ref):
    groups, rows = sums_ref.shape[0], probe_ref.shape[0]
    total = jnp.zeros((rows, LANES), jnp.float32)
    for g in range(groups):
        total = total + sums_ref[g, pl.ds(0, rows), :]
    probe_ref[...] = total * scale
    for i in range(slot_ref.shape[0]):
        slot = slot_ref[i]
        picked = sums_ref[lax.shift_right_logical(slot, 1), pl.ds(rows + (slot & 1), 1), :]
        misfit_ref[i] = jnp.sum(picked) * (1.0 / pixels)


SMEM = pl.BlockSpec(memory_space=pltpu.SMEM)
VMEM = pl.BlockSpec(memory_space=pltpu.VMEM)
ANY = pl.BlockSpec(memory_space=pl.ANY)


def local(obj, probe, measured, tile_of, inner):
    cols_along = lax.axis_size("ty")
    groups = lax.axis_size("tx") * cols_along
    depth = lax.axis_size("pos")
    modes, _, width, _ = probe.shape
    tile_width = obj.shape[-1]
    blocks = tile_width // LANES
    per_device = measured.shape[0]
    positions = per_device * groups * depth
    slots = groups * CAP
    plane = ("tx", "ty")
    my_tile = lax.axis_index("tx") * cols_along + lax.axis_index("ty")
    where = jnp.stack([my_tile, lax.axis_index("pos")]).astype(jnp.int32)
    packed = (tile_of[:, 0] << TILE_SHIFT) | (inner[:, 0] << ROW_BITS) | inner[:, 1]
    sizes = (groups, depth, per_device)

    outgoing, own_slots = pl.pallas_call(
        lambda *refs: send_kernel(*sizes, *refs),
        out_shape=(
            jax.ShapeDtypeStruct((slots, width, width), measured.dtype),
            jax.ShapeDtypeStruct((per_device,), jnp.int32),
        ),
        in_specs=[SMEM, SMEM, ANY],
        out_specs=(ANY, SMEM),
        scratch_shapes=[pltpu.SemaphoreType.DMA((per_device,))],
        name="send_slots",
    )(where, packed, measured)
    arrived = lax.all_to_all(
        outgoing.reshape(groups, CAP, width, width), plane, split_axis=0, concat_axis=0, tiled=True
    ).reshape(slots, width, width)
    listed = pl.pallas_call(
        lambda *refs: list_kernel(*sizes, *refs),
        out_shape=jax.ShapeDtypeStruct((slots + 8,), jnp.int32),
        in_specs=[SMEM, SMEM],
        out_specs=SMEM,
        cost_estimate=pl.CostEstimate(flops=10_000_000, bytes_accessed=10_000_000, transcendentals=0),
        name="list_windows",
    )(where, packed)
    x_table, y_table = dft_blocks(width)
    rows = modes * 2 * width // groups
    tile_grad, sums = pl.pallas_call(
        lambda *refs: main_kernel(modes, slots, *refs),
        out_shape=(
            jax.ShapeDtypeStruct(obj.shape, jnp.float32),
            jax.ShapeDtypeStruct((groups, rows + 8, LANES), jnp.float32),
        ),
        in_specs=[SMEM, ANY, VMEM, ANY, VMEM, VMEM],
        out_specs=(ANY, VMEM),
        scratch_shapes=[
            pltpu.VMEM((2, blocks, tile_width, LANES), jnp.float32),
            pltpu.VMEM((2, blocks, tile_width, LANES), jnp.float32),
            pltpu.VMEM((modes, 2, width, LANES), jnp.float32),
            pltpu.VMEM((slots, width, width), measured.dtype),
            pltpu.VMEM((slots, 1, LANES), jnp.float32),
            pltpu.SemaphoreType.DMA((2 * blocks + 1,)),
        ],
        compiler_params=pltpu.CompilerParams(vmem_limit_bytes=48 << 20),
        name="windows",
    )(listed, obj, probe, arrived, jnp.asarray(x_table), jnp.asarray(y_table))
    shares = lax.psum_scatter(tile_grad, "pos", scatter_dimension=1, tiled=True)
    sums = lax.all_to_all(sums, plane, split_axis=0, concat_axis=0, tiled=True)
    probe_part, misfit = pl.pallas_call(
        lambda *refs: receive_kernel(1.0 / positions, width * width, *refs),
        out_shape=(
            jax.ShapeDtypeStruct((rows, LANES), jnp.float32),
            jax.ShapeDtypeStruct((per_device,), jnp.float32),
        ),
        in_specs=[SMEM, VMEM],
        out_specs=(VMEM, SMEM),
        name="receive_sums",
    )(own_slots, sums)
    probe_part = jnp.sum(lax.all_gather(probe_part, "pos", axis=0), axis=0)
    probe_total = lax.all_gather(probe_part, plane, axis=0, tiled=True)
    return (shares, probe_total.reshape(modes, 2, width, width), misfit)


def solution(mesh):
    return jax.shard_map(
        local,
        mesh=mesh,
        in_specs=(P(None, "tx", "ty"), P(), P(("tx", "ty", "pos"), None, None), P(), P()),
        out_specs=(P(None, ("tx", "pos"), "ty"), P(), P(("tx", "ty", "pos"))),
        check_vma=False,
    )
```

```python
import jax
import jax.numpy as jnp
import ml_dtypes
import numpy as np
from jax import lax
from jax.experimental import pallas as pl
from jax.experimental.pallas import tpu as pltpu
from jax.sharding import PartitionSpec as P

CAP = 2
UNROLL = 2
LANES = 128
ROW_BITS = 10
TILE_SHIFT = 2 * ROW_BITS
LOW = (1 << ROW_BITS) - 1


def dft_blocks(width):
    counter = np.arange(width, dtype=np.int32)
    product = counter[:, None] * counter[None, :] % width
    angles = product.astype(np.float32) * np.float32(2.0 * np.pi / width)
    factor = np.float32(1.0) / np.sqrt(np.float32(width))
    c = (np.cos(angles) * factor).astype(ml_dtypes.bfloat16)
    s = (-np.sin(angles) * factor).astype(ml_dtypes.bfloat16)
    return np.block([[c, -s], [s, c]]), np.block([[c, s], [-s, c]])


def send_kernel(groups, depth, per_device, where_ref, packed_ref, measured_ref, out_ref, slot_ref):
    base = (where_ref[0] * depth + where_ref[1]) * per_device
    tiles = [lax.shift_right_logical(packed_ref[base + i], TILE_SHIFT) for i in range(per_device)]
    for i in range(per_device):
        rank = jnp.int32(0)
        for j in range(i):
            rank = rank + (tiles[j] == tiles[i]).astype(jnp.int32)
        slot = tiles[i] * CAP + rank
        slot_ref[i] = slot
        out_ref[slot] = measured_ref[i]


def list_kernel(groups, depth, per_device, where_ref, packed_ref, list_ref):
    tile = where_ref[0]
    plane = where_ref[1]

    def one_group(group, count):
        base = (group * depth + plane) * per_device
        rank = jnp.int32(0)
        for i in range(per_device):
            value = packed_ref[base + i]
            hit = (lax.shift_right_logical(value, TILE_SHIFT) == tile).astype(jnp.int32)
            slot = group * CAP + rank
            list_ref[count] = (slot << TILE_SHIFT) | (value & ((1 << TILE_SHIFT) - 1))
            count = count + hit
            rank = rank + hit
        return count

    count = lax.fori_loop(0, groups, one_group, jnp.int32(0))
    for u in range(UNROLL - 1):
        list_ref[count + u] = jnp.int32((groups * CAP) << TILE_SHIFT)
    list_ref[groups * CAP + UNROLL] = (count + UNROLL - 1) // UNROLL


def window_of(entry, blocks):
    slot = lax.shift_right_logical(entry, TILE_SHIFT)
    row = lax.shift_right_logical(entry, ROW_BITS) & LOW
    col = entry & LOW
    block = jnp.minimum(lax.shift_right_logical(col, 7), blocks - 2)
    return slot, row, block, col - block * LANES


def stack(half, width):
    fields = half.shape[0] // width
    columns = []
    for f in range(fields):
        rows = half[f * width : (f + 1) * width]
        columns.append(jnp.concatenate([rows[:, :width], rows[:, width:]], axis=0))
    return jnp.concatenate(columns, axis=1)


def forward_kernel(
    slots,
    list_ref,
    obj_ref,
    probe_ref,
    x_ref,
    y_ref,
    far_ref,
    patch_ref,
    tile_s,
    far_s,
    patch_s,
    sems,
    out_sems,
):
    width = LANES
    modes = probe_ref.shape[0]
    blocks = tile_s.shape[1]
    steps = list_ref[slots + UNROLL]
    copies = [
        pltpu.make_async_copy(
            obj_ref.at[a, :, pl.ds(b * LANES, LANES)], tile_s.at[a, b], sems.at[a * blocks + b]
        )
        for a in range(2)
        for b in range(blocks)
    ]
    for copy in copies:
        copy.start()
    for copy in copies:
        copy.wait()

    def leaving(n):
        turn = n & 1
        there = pl.ds(n * UNROLL, UNROLL)
        return (
            pltpu.make_async_copy(far_s.at[turn], far_ref.at[there], out_sems.at[0, turn]),
            pltpu.make_async_copy(patch_s.at[turn], patch_ref.at[there], out_sems.at[1, turn]),
        )

    lane = lax.broadcasted_iota(jnp.int32, (width, LANES), 1)

    def step(n, carry):
        turn = n & 1

        @pl.when(n >= 2)
        def _():
            for copy in leaving(n - 2):
                copy.wait()

        waves = []
        for u in range(UNROLL):
            _, row, block, shift = window_of(list_ref[n * UNROLL + u], blocks)
            back_shift = (LANES - shift) & (LANES - 1)
            own = lane < LANES - shift
            parts = []
            for a in range(2):
                left = pltpu.roll(tile_s[a, block, pl.ds(row, width), :], back_shift, 1)
                right = pltpu.roll(tile_s[a, block + 1, pl.ds(row, width), :], back_shift, 1)
                rounded = jnp.where(own, left, right).astype(jnp.bfloat16)
                patch_s[turn, u, a] = rounded
                parts.append(rounded.astype(jnp.float32))
            obj_r, obj_i = parts
            for k in range(modes):
                p_r = probe_ref[k, 0]
                p_i = probe_ref[k, 1]
                waves.append(
                    jnp.concatenate(
                        [p_r * obj_r - p_i * obj_i, p_r * obj_i + p_i * obj_r], axis=1
                    ).astype(jnp.bfloat16)
                )
        half = jnp.dot(jnp.concatenate(waves, axis=0), y_ref[...], preferred_element_type=jnp.float32)
        far = jnp.dot(
            x_ref[...], stack(half.astype(jnp.bfloat16), width), preferred_element_type=jnp.float32
        )
        for u in range(UNROLL):
            far_s[turn, u] = far[:, u * modes * width : (u + 1) * modes * width]
        for copy in leaving(n):
            copy.start()
        return carry

    lax.fori_loop(0, steps, step, jnp.int32(0))
    for late in (2, 1):

        @pl.when(steps >= late)
        def _():
            for copy in leaving(steps - late):
                copy.wait()


def backward_kernel(
    slots,
    list_ref,
    far_ref,
    patch_ref,
    probe_ref,
    meas_ref,
    x_ref,
    y_ref,
    grad_ref,
    sums_ref,
    acc_s,
    probe_s,
    misfit_s,
    far_s,
    patch_s,
    sems,
    in_sems,
):
    width = LANES
    modes = probe_ref.shape[0]
    blocks = acc_s.shape[1]
    steps = list_ref[slots + UNROLL]

    def coming(n):
        turn = n & 1
        there = pl.ds(n * UNROLL, UNROLL)
        return (
            pltpu.make_async_copy(far_ref.at[there], far_s.at[turn], in_sems.at[0, turn]),
            pltpu.make_async_copy(patch_ref.at[there], patch_s.at[turn], in_sems.at[1, turn]),
        )

    @pl.when(steps > 0)
    def _():
        for copy in coming(0):
            copy.start()

    acc_s[...] = jnp.zeros_like(acc_s)
    probe_s[...] = jnp.zeros_like(probe_s)
    misfit_s[...] = jnp.zeros_like(misfit_s)
    lane = lax.broadcasted_iota(jnp.int32, (width, LANES), 1)

    def step(n, carry):
        turn = n & 1

        @pl.when(n + 1 < steps)
        def _():
            for copy in coming(n + 1):
                copy.start()

        for copy in coming(n):
            copy.wait()
        entries = [list_ref[n * UNROLL + u] for u in range(UNROLL)]
        residuals = []
        for u in range(UNROLL):
            slot = lax.shift_right_logical(entries[u], TILE_SHIFT)
            intensity = jnp.ones((width, LANES), jnp.float32)
            for k in range(modes):
                f_r = far_s[turn, u, pl.ds(0, width), pl.ds(k * width, width)]
                f_i = far_s[turn, u, pl.ds(width, width), pl.ds(k * width, width)]
                intensity = intensity + (f_r * f_r + f_i * f_i)
            data = meas_ref[jnp.minimum(slot, slots - 1)].astype(jnp.float32)
            inverse = lax.rsqrt(intensity)
            gap = intensity * inverse - data
            misfit_s[slot] = jnp.sum(gap * gap, axis=0, keepdims=True)
            factor = jnp.where(slot < slots, 1.0 - data * inverse, 0.0)
            for k in range(modes):
                f_r = far_s[turn, u, pl.ds(0, width), pl.ds(k * width, width)]
                f_i = far_s[turn, u, pl.ds(width, width), pl.ds(k * width, width)]
                residuals.append(jnp.concatenate([f_r * factor, f_i * factor], axis=1).astype(jnp.bfloat16))
        half = jnp.dot(jnp.concatenate(residuals, axis=0), x_ref[...], preferred_element_type=jnp.float32)
        back = jnp.dot(
            y_ref[...], stack(half.astype(jnp.bfloat16), width), preferred_element_type=jnp.float32
        )
        objs = [[patch_s[turn, u, a].astype(jnp.float32) for a in range(2)] for u in range(UNROLL)]
        parts = [[0.0, 0.0] for _ in range(UNROLL)]
        for k in range(modes):
            p_r = probe_ref[k, 0]
            p_i = probe_ref[k, 1]
            sum_r = probe_s[k, 0]
            sum_i = probe_s[k, 1]
            for u in range(UNROLL):
                at = (u * modes + k) * width
                b_r = back[:width, at : at + width]
                b_i = back[width:, at : at + width]
                obj_r, obj_i = objs[u]
                parts[u][0] = parts[u][0] + (p_r * b_r + p_i * b_i)
                parts[u][1] = parts[u][1] + (p_r * b_i - p_i * b_r)
                sum_r = sum_r + (obj_r * b_r + obj_i * b_i)
                sum_i = sum_i + (obj_r * b_i - obj_i * b_r)
            probe_s[k, 0] = sum_r
            probe_s[k, 1] = sum_i
        for u in range(UNROLL):
            _, row, block, shift = window_of(entries[u], blocks)
            keep = lane >= shift
            for a in range(2):
                turned = pltpu.roll(parts[u][a], shift & (LANES - 1), 1)
                spot = (a, block, pl.ds(row, width), slice(None))
                acc_s[spot] = acc_s[spot] + jnp.where(keep, turned, 0.0)
                spot = (a, block + 1, pl.ds(row, width), slice(None))
                acc_s[spot] = acc_s[spot] + jnp.where(keep, 0.0, turned)
        return carry

    lax.fori_loop(0, steps, step, jnp.int32(0))
    groups = sums_ref.shape[0]
    rows = sums_ref.shape[1] - 8
    copies = [
        pltpu.make_async_copy(
            acc_s.at[a, b], grad_ref.at[a, :, pl.ds(b * LANES, LANES)], sems.at[a * blocks + b]
        )
        for a in range(2)
        for b in range(blocks)
    ]
    for copy in copies:
        copy.start()
    per_plane = width // rows
    for g in range(groups):
        plane, part = divmod(g, per_plane)
        sums_ref[g, pl.ds(0, rows), :] = probe_s[plane // 2, plane % 2, pl.ds(part * rows, rows), :]
        for s in range(CAP):
            sums_ref[g, pl.ds(rows + s, 1), :] = misfit_s[g * CAP + s]
        sums_ref[g, pl.ds(rows + CAP, 8 - CAP), :] = jnp.zeros((8 - CAP, LANES), jnp.float32)
    for copy in copies:
        copy.wait()


def receive_kernel(scale, pixels, slot_ref, sums_ref, probe_ref, misfit_ref):
    groups, rows = sums_ref.shape[0], probe_ref.shape[0]
    total = jnp.zeros((rows, LANES), jnp.float32)
    for g in range(groups):
        total = total + sums_ref[g, pl.ds(0, rows), :]
    probe_ref[...] = total * scale
    for i in range(slot_ref.shape[0]):
        slot = slot_ref[i]
        picked = sums_ref[lax.shift_right_logical(slot, 1), pl.ds(rows + (slot & 1), 1), :]
        misfit_ref[i] = jnp.sum(picked) * (1.0 / pixels)


SMEM = pl.BlockSpec(memory_space=pltpu.SMEM)
VMEM = pl.BlockSpec(memory_space=pltpu.VMEM)
ANY = pl.BlockSpec(memory_space=pl.ANY)


def local(obj, probe, measured, tile_of, inner):
    cols_along = lax.axis_size("ty")
    groups = lax.axis_size("tx") * cols_along
    depth = lax.axis_size("pos")
    modes, _, width, _ = probe.shape
    tile_width = obj.shape[-1]
    blocks = tile_width // LANES
    per_device = measured.shape[0]
    positions = per_device * groups * depth
    slots = groups * CAP
    plane = ("tx", "ty")
    my_tile = lax.axis_index("tx") * cols_along + lax.axis_index("ty")
    where = jnp.stack([my_tile, lax.axis_index("pos")]).astype(jnp.int32)
    packed = (tile_of[:, 0] << TILE_SHIFT) | (inner[:, 0] << ROW_BITS) | inner[:, 1]
    sizes = (groups, depth, per_device)

    outgoing, own_slots = pl.pallas_call(
        lambda *refs: send_kernel(*sizes, *refs),
        out_shape=(
            jax.ShapeDtypeStruct((slots, width, width), measured.dtype),
            jax.ShapeDtypeStruct((per_device,), jnp.int32),
        ),
        in_specs=[SMEM, SMEM, VMEM],
        out_specs=(VMEM, SMEM),
        name="send_slots",
    )(where, packed, measured)
    arrived = lax.all_to_all(
        outgoing.reshape(groups, CAP, width, width), plane, split_axis=0, concat_axis=0, tiled=True
    ).reshape(slots, width, width)
    listed = pl.pallas_call(
        lambda *refs: list_kernel(*sizes, *refs),
        out_shape=jax.ShapeDtypeStruct((slots + 2 * UNROLL + 4,), jnp.int32),
        in_specs=[SMEM, SMEM],
        out_specs=SMEM,
        cost_estimate=pl.CostEstimate(flops=1_000_000, bytes_accessed=10_000_000, transcendentals=0),
        name="list_windows",
    )(where, packed)
    tables = [jnp.asarray(table) for table in dft_blocks(width)]
    rows = modes * 2 * width // groups
    flops = slots // 2 * modes * 2 * (2 * width) ** 2 * width * 2
    staging = [
        pltpu.VMEM((2, UNROLL, 2 * width, modes * width), jnp.float32),
        pltpu.VMEM((2, UNROLL, 2, width, width), jnp.bfloat16),
    ]
    far, patches = pl.pallas_call(
        lambda *refs: forward_kernel(slots, *refs),
        out_shape=(
            jax.ShapeDtypeStruct((slots + UNROLL, 2 * width, modes * width), jnp.float32),
            jax.ShapeDtypeStruct((slots + UNROLL, 2, width, width), jnp.bfloat16),
        ),
        in_specs=[SMEM, ANY, VMEM, VMEM, VMEM],
        out_specs=(ANY, ANY),
        scratch_shapes=[
            pltpu.VMEM((2, blocks, tile_width, LANES), jnp.float32),
            *staging,
            pltpu.SemaphoreType.DMA((2 * blocks,)),
            pltpu.SemaphoreType.DMA((2, 2)),
        ],
        compiler_params=pltpu.CompilerParams(vmem_limit_bytes=48 << 20),
        cost_estimate=pl.CostEstimate(flops=flops, bytes_accessed=40_000_000, transcendentals=0),
        name="forward_windows",
    )(listed, obj, probe, *tables)
    tile_grad, sums = pl.pallas_call(
        lambda *refs: backward_kernel(slots, *refs),
        out_shape=(
            jax.ShapeDtypeStruct(obj.shape, jnp.float32),
            jax.ShapeDtypeStruct((groups, rows + 8, LANES), jnp.float32),
        ),
        in_specs=[SMEM, ANY, ANY, VMEM, VMEM, VMEM, VMEM],
        out_specs=(ANY, VMEM),
        scratch_shapes=[
            pltpu.VMEM((2, blocks, tile_width, LANES), jnp.float32),
            pltpu.VMEM((modes, 2, width, LANES), jnp.float32),
            pltpu.VMEM((slots + 1, 1, LANES), jnp.float32),
            *staging,
            pltpu.SemaphoreType.DMA((2 * blocks,)),
            pltpu.SemaphoreType.DMA((2, 2)),
        ],
        compiler_params=pltpu.CompilerParams(vmem_limit_bytes=48 << 20),
        cost_estimate=pl.CostEstimate(flops=flops, bytes_accessed=40_000_000, transcendentals=0),
        name="backward_windows",
    )(listed, far, patches, probe, arrived, *tables)
    shares = lax.psum_scatter(tile_grad, "pos", scatter_dimension=1, tiled=True)
    sums = lax.all_to_all(sums, plane, split_axis=0, concat_axis=0, tiled=True)
    probe_part, misfit = pl.pallas_call(
        lambda *refs: receive_kernel(1.0 / positions, width * width, *refs),
        out_shape=(
            jax.ShapeDtypeStruct((rows, LANES), jnp.float32),
            jax.ShapeDtypeStruct((per_device,), jnp.float32),
        ),
        in_specs=[SMEM, VMEM],
        out_specs=(VMEM, SMEM),
        name="receive_sums",
    )(own_slots, sums)
    probe_part = jnp.sum(lax.all_gather(probe_part, "pos", axis=0), axis=0)
    probe_total = lax.all_gather(probe_part, plane, axis=0, tiled=True)
    return (shares, probe_total.reshape(modes, 2, width, width), misfit)


def solution(mesh):
    return jax.shard_map(
        local,
        mesh=mesh,
        in_specs=(P(None, "tx", "ty"), P(), P(("tx", "ty", "pos"), None, None), P(), P()),
        out_specs=(P(None, ("tx", "pos"), "ty"), P(), P(("tx", "ty", "pos"))),
        check_vma=False,
    )
```

```python
import jax
import jax.numpy as jnp
import ml_dtypes
import numpy as np
from jax import lax
from jax.experimental import pallas as pl
from jax.experimental.pallas import tpu as pltpu
from jax.sharding import PartitionSpec as P

CAP = 2
UNROLL = 2
LANES = 128
ROW_BITS = 10
TILE_SHIFT = 2 * ROW_BITS
LOW = (1 << ROW_BITS) - 1


def dft_blocks(width):
    counter = np.arange(width, dtype=np.int32)
    product = counter[:, None] * counter[None, :] % width
    angles = product.astype(np.float32) * np.float32(2.0 * np.pi / width)
    factor = np.float32(1.0) / np.sqrt(np.float32(width))
    c = (np.cos(angles) * factor).astype(ml_dtypes.bfloat16)
    s = (-np.sin(angles) * factor).astype(ml_dtypes.bfloat16)
    return np.block([[c, -s], [s, c]]), np.block([[c, s], [-s, c]])


def send_kernel(groups, depth, per_device, where_ref, packed_ref, measured_ref, out_ref, slot_ref):
    base = (where_ref[0] * depth + where_ref[1]) * per_device
    tiles = [lax.shift_right_logical(packed_ref[base + i], TILE_SHIFT) for i in range(per_device)]
    for i in range(per_device):
        rank = jnp.int32(0)
        for j in range(i):
            rank = rank + (tiles[j] == tiles[i]).astype(jnp.int32)
        slot = tiles[i] * CAP + rank
        slot_ref[i] = slot
        out_ref[slot] = measured_ref[i]


def list_kernel(groups, depth, per_device, where_ref, packed_ref, list_ref):
    tile = where_ref[0]
    plane = where_ref[1]

    def one_group(group, count):
        base = (group * depth + plane) * per_device
        rank = jnp.int32(0)
        for i in range(per_device):
            value = packed_ref[base + i]
            hit = (lax.shift_right_logical(value, TILE_SHIFT) == tile).astype(jnp.int32)
            slot = group * CAP + rank
            list_ref[count] = (slot << TILE_SHIFT) | (value & ((1 << TILE_SHIFT) - 1))
            count = count + hit
            rank = rank + hit
        return count

    count = lax.fori_loop(0, groups, one_group, jnp.int32(0))
    for u in range(UNROLL - 1):
        list_ref[count + u] = jnp.int32((groups * CAP) << TILE_SHIFT)
    list_ref[groups * CAP + UNROLL] = (count + UNROLL - 1) // UNROLL


def window_of(entry, blocks):
    slot = lax.shift_right_logical(entry, TILE_SHIFT)
    row = lax.shift_right_logical(entry, ROW_BITS) & LOW
    col = entry & LOW
    block = jnp.minimum(lax.shift_right_logical(col, 7), blocks - 2)
    return slot, row, block, col - block * LANES


def stack(half, width):
    fields = half.shape[0] // width
    columns = []
    for f in range(fields):
        rows = half[f * width : (f + 1) * width]
        columns.append(jnp.concatenate([rows[:, :width], rows[:, width:]], axis=0))
    return jnp.concatenate(columns, axis=1)


def forward_kernel(
    slots,
    list_ref,
    obj_ref,
    probe_ref,
    x_ref,
    y_ref,
    far_ref,
    patch_ref,
    tile_s,
    far_s,
    patch_s,
    sems,
    out_sems,
):
    width = LANES
    modes = probe_ref.shape[0]
    blocks = tile_s.shape[1]
    steps = list_ref[slots + UNROLL]
    copies = [
        pltpu.make_async_copy(
            obj_ref.at[a, :, pl.ds(b * LANES, LANES)], tile_s.at[a, b], sems.at[a * blocks + b]
        )
        for a in range(2)
        for b in range(blocks)
    ]
    for copy in copies:
        copy.start()
    for copy in copies:
        copy.wait()

    def leaving(n):
        turn = n & 1
        there = pl.ds(n * UNROLL, UNROLL)
        return (
            pltpu.make_async_copy(far_s.at[turn], far_ref.at[there], out_sems.at[0, turn]),
            pltpu.make_async_copy(patch_s.at[turn], patch_ref.at[there], out_sems.at[1, turn]),
        )

    lane = lax.broadcasted_iota(jnp.int32, (width, LANES), 1)

    def step(n, carry):
        turn = n & 1

        @pl.when(n >= 2)
        def _():
            for copy in leaving(n - 2):
                copy.wait()

        waves = []
        for u in range(UNROLL):
            _, row, block, shift = window_of(list_ref[n * UNROLL + u], blocks)
            back_shift = (LANES - shift) & (LANES - 1)
            own = lane < LANES - shift
            parts = []
            for a in range(2):
                left = pltpu.roll(tile_s[a, block, pl.ds(row, width), :], back_shift, 1)
                right = pltpu.roll(tile_s[a, block + 1, pl.ds(row, width), :], back_shift, 1)
                rounded = jnp.where(own, left, right).astype(jnp.bfloat16)
                patch_s[turn, u, a] = rounded
                parts.append(rounded.astype(jnp.float32))
            obj_r, obj_i = parts
            for k in range(modes):
                p_r = probe_ref[k, 0]
                p_i = probe_ref[k, 1]
                waves.append(
                    jnp.concatenate(
                        [p_r * obj_r - p_i * obj_i, p_r * obj_i + p_i * obj_r], axis=1
                    ).astype(jnp.bfloat16)
                )
        half = jnp.dot(jnp.concatenate(waves, axis=0), y_ref[...], preferred_element_type=jnp.float32)
        far = jnp.dot(
            x_ref[...], stack(half.astype(jnp.bfloat16), width), preferred_element_type=jnp.float32
        )
        for u in range(UNROLL):
            far_s[turn, u] = far[:, u * modes * width : (u + 1) * modes * width]
        for copy in leaving(n):
            copy.start()
        return carry

    lax.fori_loop(0, steps, step, jnp.int32(0))
    for late in (2, 1):

        @pl.when(steps >= late)
        def _():
            for copy in leaving(steps - late):
                copy.wait()


def backward_kernel(
    slots,
    list_ref,
    far_ref,
    patch_ref,
    probe_ref,
    meas_ref,
    x_ref,
    y_ref,
    grad_ref,
    sums_ref,
    acc_s,
    probe_s,
    misfit_s,
    far_s,
    patch_s,
    sems,
    in_sems,
):
    width = LANES
    modes = probe_ref.shape[0]
    blocks = acc_s.shape[1]
    steps = list_ref[slots + UNROLL]

    def coming(n):
        turn = n & 1
        there = pl.ds(n * UNROLL, UNROLL)
        return (
            pltpu.make_async_copy(far_ref.at[there], far_s.at[turn], in_sems.at[0, turn]),
            pltpu.make_async_copy(patch_ref.at[there], patch_s.at[turn], in_sems.at[1, turn]),
        )

    @pl.when(steps > 0)
    def _():
        for copy in coming(0):
            copy.start()

    acc_s[...] = jnp.zeros_like(acc_s)
    probe_s[...] = jnp.zeros_like(probe_s)
    misfit_s[...] = jnp.zeros_like(misfit_s)
    lane = lax.broadcasted_iota(jnp.int32, (width, LANES), 1)

    def step(n, carry):
        turn = n & 1

        @pl.when(n + 1 < steps)
        def _():
            for copy in coming(n + 1):
                copy.start()

        for copy in coming(n):
            copy.wait()
        entries = [list_ref[n * UNROLL + u] for u in range(UNROLL)]
        residuals = []
        for u in range(UNROLL):
            slot = lax.shift_right_logical(entries[u], TILE_SHIFT)
            intensity = jnp.ones((width, LANES), jnp.float32)
            for k in range(modes):
                f_r = far_s[turn, u, pl.ds(0, width), pl.ds(k * width, width)]
                f_i = far_s[turn, u, pl.ds(width, width), pl.ds(k * width, width)]
                intensity = intensity + (f_r * f_r + f_i * f_i)
            data = meas_ref[jnp.minimum(slot, slots - 1)].astype(jnp.float32)
            inverse = lax.rsqrt(intensity)
            gap = intensity * inverse - data
            misfit_s[slot] = jnp.sum(gap * gap, axis=0, keepdims=True)
            factor = jnp.where(slot < slots, 1.0 - data * inverse, 0.0)
            for k in range(modes):
                f_r = far_s[turn, u, pl.ds(0, width), pl.ds(k * width, width)]
                f_i = far_s[turn, u, pl.ds(width, width), pl.ds(k * width, width)]
                residuals.append(jnp.concatenate([f_r * factor, f_i * factor], axis=1).astype(jnp.bfloat16))
        half = jnp.dot(jnp.concatenate(residuals, axis=0), x_ref[...], preferred_element_type=jnp.float32)
        back = jnp.dot(
            y_ref[...], stack(half.astype(jnp.bfloat16), width), preferred_element_type=jnp.float32
        )
        objs = [[patch_s[turn, u, a].astype(jnp.float32) for a in range(2)] for u in range(UNROLL)]
        parts = [[0.0, 0.0] for _ in range(UNROLL)]
        for k in range(modes):
            p_r = probe_ref[k, 0]
            p_i = probe_ref[k, 1]
            sum_r = probe_s[k, 0]
            sum_i = probe_s[k, 1]
            for u in range(UNROLL):
                at = (u * modes + k) * width
                b_r = back[:width, at : at + width]
                b_i = back[width:, at : at + width]
                obj_r, obj_i = objs[u]
                parts[u][0] = parts[u][0] + (p_r * b_r + p_i * b_i)
                parts[u][1] = parts[u][1] + (p_r * b_i - p_i * b_r)
                sum_r = sum_r + (obj_r * b_r + obj_i * b_i)
                sum_i = sum_i + (obj_r * b_i - obj_i * b_r)
            probe_s[k, 0] = sum_r
            probe_s[k, 1] = sum_i
        for u in range(UNROLL):
            _, row, block, shift = window_of(entries[u], blocks)
            keep = lane >= shift
            for a in range(2):
                turned = pltpu.roll(parts[u][a], shift & (LANES - 1), 1)
                spot = (a, block, pl.ds(row, width), slice(None))
                acc_s[spot] = acc_s[spot] + jnp.where(keep, turned, 0.0)
                spot = (a, block + 1, pl.ds(row, width), slice(None))
                acc_s[spot] = acc_s[spot] + jnp.where(keep, 0.0, turned)
        return carry

    lax.fori_loop(0, steps, step, jnp.int32(0))
    groups = sums_ref.shape[0]
    rows = sums_ref.shape[1] - 8
    copies = [
        pltpu.make_async_copy(
            acc_s.at[a, b], grad_ref.at[a, :, pl.ds(b * LANES, LANES)], sems.at[a * blocks + b]
        )
        for a in range(2)
        for b in range(blocks)
    ]
    for copy in copies:
        copy.start()
    per_plane = width // rows
    for g in range(groups):
        plane, part = divmod(g, per_plane)
        sums_ref[g, pl.ds(0, rows), :] = probe_s[plane // 2, plane % 2, pl.ds(part * rows, rows), :]
        for s in range(CAP):
            sums_ref[g, pl.ds(rows + s, 1), :] = misfit_s[g * CAP + s]
        sums_ref[g, pl.ds(rows + CAP, 8 - CAP), :] = jnp.zeros((8 - CAP, LANES), jnp.float32)
    for copy in copies:
        copy.wait()


def receive_kernel(scale, pixels, slot_ref, sums_ref, probe_ref, misfit_ref):
    groups, rows = sums_ref.shape[0], probe_ref.shape[0]
    total = jnp.zeros((rows, LANES), jnp.float32)
    for g in range(groups):
        total = total + sums_ref[g, pl.ds(0, rows), :]
    probe_ref[...] = total * scale
    for i in range(slot_ref.shape[0]):
        slot = slot_ref[i]
        picked = sums_ref[lax.shift_right_logical(slot, 1), pl.ds(rows + (slot & 1), 1), :]
        misfit_ref[i] = jnp.sum(picked) * (1.0 / pixels)


SMEM = pl.BlockSpec(memory_space=pltpu.SMEM)
VMEM = pl.BlockSpec(memory_space=pltpu.VMEM)
ANY = pl.BlockSpec(memory_space=pl.ANY)


def kernels(tile_shape, modes, width, slots, per_device, groups):
    tile_width = tile_shape[-1]
    blocks = tile_width // LANES
    rows = modes * 2 * width // groups
    flops = slots // 2 * modes * 2 * (2 * width) ** 2 * width * 2
    staging = [
        pltpu.VMEM((2, UNROLL, 2 * width, modes * width), jnp.float32),
        pltpu.VMEM((2, UNROLL, 2, width, width), jnp.bfloat16),
    ]
    forward = pl.pallas_call(
        lambda *refs: forward_kernel(slots, *refs),
        out_shape=(
            jax.ShapeDtypeStruct((slots + UNROLL, 2 * width, modes * width), jnp.float32),
            jax.ShapeDtypeStruct((slots + UNROLL, 2, width, width), jnp.bfloat16),
        ),
        in_specs=[SMEM, ANY, VMEM, VMEM, VMEM],
        out_specs=(ANY, ANY),
        scratch_shapes=[
            pltpu.VMEM((2, blocks, tile_width, LANES), jnp.float32),
            *staging,
            pltpu.SemaphoreType.DMA((2 * blocks,)),
            pltpu.SemaphoreType.DMA((2, 2)),
        ],
        compiler_params=pltpu.CompilerParams(vmem_limit_bytes=48 << 20),
        cost_estimate=pl.CostEstimate(flops=flops, bytes_accessed=40_000_000, transcendentals=0),
        name="forward_windows",
    )
    backward = pl.pallas_call(
        lambda *refs: backward_kernel(slots, *refs),
        out_shape=(
            jax.ShapeDtypeStruct(tile_shape, jnp.float32),
            jax.ShapeDtypeStruct((groups, rows + 8, LANES), jnp.float32),
        ),
        in_specs=[SMEM, ANY, ANY, VMEM, VMEM, VMEM, VMEM],
        out_specs=(ANY, VMEM),
        scratch_shapes=[
            pltpu.VMEM((2, blocks, tile_width, LANES), jnp.float32),
            pltpu.VMEM((modes, 2, width, LANES), jnp.float32),
            pltpu.VMEM((slots + 1, 1, LANES), jnp.float32),
            *staging,
            pltpu.SemaphoreType.DMA((2 * blocks,)),
            pltpu.SemaphoreType.DMA((2, 2)),
        ],
        compiler_params=pltpu.CompilerParams(vmem_limit_bytes=48 << 20),
        cost_estimate=pl.CostEstimate(flops=flops, bytes_accessed=40_000_000, transcendentals=0),
        name="backward_windows",
    )
    return forward, backward


def local(obj, probe, measured, tile_of, inner):
    cols_along = lax.axis_size("ty")
    groups = lax.axis_size("tx") * cols_along
    depth = lax.axis_size("pos")
    modes, _, width, _ = probe.shape
    per_device = measured.shape[0]
    positions = per_device * groups * depth
    slots = groups * CAP
    plane = ("tx", "ty")
    my_tile = lax.axis_index("tx") * cols_along + lax.axis_index("ty")
    where = jnp.stack([my_tile, lax.axis_index("pos")]).astype(jnp.int32)
    packed = (tile_of[:, 0] << TILE_SHIFT) | (inner[:, 0] << ROW_BITS) | inner[:, 1]
    sizes = (groups, depth, per_device)

    outgoing, own_slots = pl.pallas_call(
        lambda *refs: send_kernel(*sizes, *refs),
        out_shape=(
            jax.ShapeDtypeStruct((slots, width, width), measured.dtype),
            jax.ShapeDtypeStruct((per_device,), jnp.int32),
        ),
        in_specs=[SMEM, SMEM, VMEM],
        out_specs=(VMEM, SMEM),
        name="send_slots",
    )(where, packed, measured)
    arrived = lax.all_to_all(
        outgoing.reshape(groups, CAP, width, width), plane, split_axis=0, concat_axis=0, tiled=True
    ).reshape(slots, width, width)
    listed = pl.pallas_call(
        lambda *refs: list_kernel(*sizes, *refs),
        out_shape=jax.ShapeDtypeStruct((slots + 2 * UNROLL + 4,), jnp.int32),
        in_specs=[SMEM, SMEM],
        out_specs=SMEM,
        cost_estimate=pl.CostEstimate(flops=1_000_000, bytes_accessed=10_000_000, transcendentals=0),
        name="list_windows",
    )(where, packed)
    tables = [jnp.asarray(table) for table in dft_blocks(width)]
    rows = modes * 2 * width // groups
    forward, backward = kernels(obj.shape, modes, width, slots, per_device, groups)
    far, patches = forward(listed, obj, probe, *tables)
    tile_grad, sums = backward(listed, far, patches, probe, arrived, *tables)
    shares = lax.psum_scatter(tile_grad, "pos", scatter_dimension=1, tiled=True)
    sums = lax.all_to_all(sums, plane, split_axis=0, concat_axis=0, tiled=True)
    probe_part, misfit = pl.pallas_call(
        lambda *refs: receive_kernel(1.0 / positions, width * width, *refs),
        out_shape=(
            jax.ShapeDtypeStruct((rows, LANES), jnp.float32),
            jax.ShapeDtypeStruct((per_device,), jnp.float32),
        ),
        in_specs=[SMEM, VMEM],
        out_specs=(VMEM, SMEM),
        name="receive_sums",
    )(own_slots, sums)
    probe_part = jnp.sum(lax.all_gather(probe_part, "pos", axis=0), axis=0)
    probe_total = lax.all_gather(probe_part, plane, axis=0, tiled=True)
    return (shares, probe_total.reshape(modes, 2, width, width), misfit)


def solution(mesh):
    return jax.shard_map(
        local,
        mesh=mesh,
        in_specs=(P(None, "tx", "ty"), P(), P(("tx", "ty", "pos"), None, None), P(), P()),
        out_specs=(P(None, ("tx", "pos"), "ty"), P(), P(("tx", "ty", "pos"))),
        check_vma=False,
    )
```

```python
import jax
import jax.numpy as jnp
import ml_dtypes
import numpy as np
from jax import lax
from jax.experimental import pallas as pl
from jax.experimental.pallas import tpu as pltpu
from jax.sharding import PartitionSpec as P

CAP = 2
UNROLL = 4
STRIP = 16
LANES = 128
ROW_BITS = 10
TILE_SHIFT = 2 * ROW_BITS
LOW = (1 << ROW_BITS) - 1


def dft_blocks(width):
    counter = np.arange(width, dtype=np.int32)
    product = counter[:, None] * counter[None, :] % width
    angles = product.astype(np.float32) * np.float32(2.0 * np.pi / width)
    factor = np.float32(1.0) / np.sqrt(np.float32(width))
    c = (np.cos(angles) * factor).astype(ml_dtypes.bfloat16)
    s = (-np.sin(angles) * factor).astype(ml_dtypes.bfloat16)
    return np.block([[c, -s], [s, c]]), np.block([[c, s], [-s, c]])


def send_kernel(groups, depth, per_device, where_ref, packed_ref, measured_ref, out_ref, slot_ref):
    base = (where_ref[0] * depth + where_ref[1]) * per_device
    tiles = [lax.shift_right_logical(packed_ref[base + i], TILE_SHIFT) for i in range(per_device)]
    for i in range(per_device):
        rank = jnp.int32(0)
        for j in range(i):
            rank = rank + (tiles[j] == tiles[i]).astype(jnp.int32)
        slot = tiles[i] * CAP + rank
        slot_ref[i] = slot
        out_ref[slot] = measured_ref[i]


def list_kernel(groups, depth, per_device, where_ref, packed_ref, list_ref):
    tile = where_ref[0]
    plane = where_ref[1]

    def one_group(group, count):
        base = (group * depth + plane) * per_device
        rank = jnp.int32(0)
        for i in range(per_device):
            value = packed_ref[base + i]
            hit = (lax.shift_right_logical(value, TILE_SHIFT) == tile).astype(jnp.int32)
            slot = group * CAP + rank
            list_ref[count] = (slot << TILE_SHIFT) | (value & ((1 << TILE_SHIFT) - 1))
            count = count + hit
            rank = rank + hit
        return count

    count = lax.fori_loop(0, groups, one_group, jnp.int32(0))
    for u in range(UNROLL - 1):
        list_ref[count + u] = jnp.int32((groups * CAP) << TILE_SHIFT)
    list_ref[groups * CAP + UNROLL] = (count + UNROLL - 1) // UNROLL


def window_of(entry, blocks):
    slot = lax.shift_right_logical(entry, TILE_SHIFT)
    row = lax.shift_right_logical(entry, ROW_BITS) & LOW
    col = entry & LOW
    block = jnp.minimum(lax.shift_right_logical(col, 7), blocks - 2)
    return slot, row, block, col - block * LANES


def right_product(field_s, table_ref, half_s, u):
    width = LANES
    half = jnp.dot(field_s[u], table_ref[...], preferred_element_type=jnp.float32)
    for k in range(field_s.shape[1] // width):
        for h in range(2):
            half_s[u, pl.ds(h * width, width), pl.ds(k * width, width)] = half[
                k * width : (k + 1) * width, h * width : (h + 1) * width
            ].astype(jnp.bfloat16)


def forward_kernel(
    slots,
    list_ref,
    obj_ref,
    probe_ref,
    x_ref,
    y_ref,
    far_ref,
    patch_ref,
    tile_s,
    far_s,
    patch_s,
    field_s,
    half_s,
    sems,
    out_sems,
):
    width = LANES
    modes = probe_ref.shape[0]
    blocks = tile_s.shape[1]
    steps = list_ref[slots + UNROLL]
    copies = [
        pltpu.make_async_copy(
            obj_ref.at[a, :, pl.ds(b * LANES, LANES)], tile_s.at[a, b], sems.at[a * blocks + b]
        )
        for a in range(2)
        for b in range(blocks)
    ]
    for copy in copies:
        copy.start()
    for copy in copies:
        copy.wait()

    def leaving(n):
        turn = n & 1
        there = pl.ds(n * UNROLL, UNROLL)
        return (
            pltpu.make_async_copy(far_s.at[turn], far_ref.at[there], out_sems.at[0, turn]),
            pltpu.make_async_copy(patch_s.at[turn], patch_ref.at[there], out_sems.at[1, turn]),
        )

    lane = lax.broadcasted_iota(jnp.int32, (STRIP, LANES), 1)

    def step(n, carry):
        turn = n & 1

        @pl.when(n >= 2)
        def _():
            for copy in leaving(n - 2):
                copy.wait()

        places = [window_of(list_ref[n * UNROLL + u], blocks) for u in range(UNROLL)]
        for s in range(0, width, STRIP):
            objs = []
            for u in range(UNROLL):
                _, row, block, shift = places[u]
                back_shift = (LANES - shift) & (LANES - 1)
                own = lane < LANES - shift
                parts = []
                for a in range(2):
                    left = pltpu.roll(tile_s[a, block, pl.ds(row + s, STRIP), :], back_shift, 1)
                    right = pltpu.roll(tile_s[a, block + 1, pl.ds(row + s, STRIP), :], back_shift, 1)
                    rounded = jnp.where(own, left, right).astype(jnp.bfloat16)
                    patch_s[turn, u, a, pl.ds(s, STRIP), :] = rounded
                    parts.append(rounded.astype(jnp.float32))
                objs.append(parts)
            for k in range(modes):
                p_r = probe_ref[k, 0, pl.ds(s, STRIP), :]
                p_i = probe_ref[k, 1, pl.ds(s, STRIP), :]
                for u in range(UNROLL):
                    o_r, o_i = objs[u]
                    at = pl.ds(k * width + s, STRIP)
                    field_s[u, at, pl.ds(0, width)] = (p_r * o_r - p_i * o_i).astype(jnp.bfloat16)
                    field_s[u, at, pl.ds(width, width)] = (p_r * o_i + p_i * o_r).astype(jnp.bfloat16)
        for u in range(UNROLL):
            right_product(field_s, y_ref, half_s, u)
        for u in range(UNROLL):
            far_s[turn, u] = jnp.dot(x_ref[...], half_s[u], preferred_element_type=jnp.float32)
        for copy in leaving(n):
            copy.start()
        return carry

    lax.fori_loop(0, steps, step, jnp.int32(0))
    for late in (2, 1):

        @pl.when(steps >= late)
        def _():
            for copy in leaving(steps - late):
                copy.wait()


def backward_kernel(
    slots,
    list_ref,
    far_ref,
    patch_ref,
    probe_ref,
    meas_ref,
    x_ref,
    y_ref,
    grad_ref,
    sums_ref,
    acc_s,
    probe_s,
    misfit_s,
    far_s,
    patch_s,
    field_s,
    half_s,
    back_s,
    sems,
    in_sems,
):
    width = LANES
    modes = probe_ref.shape[0]
    blocks = acc_s.shape[1]
    steps = list_ref[slots + UNROLL]

    def coming(n):
        turn = n & 1
        there = pl.ds(n * UNROLL, UNROLL)
        return (
            pltpu.make_async_copy(far_ref.at[there], far_s.at[turn], in_sems.at[0, turn]),
            pltpu.make_async_copy(patch_ref.at[there], patch_s.at[turn], in_sems.at[1, turn]),
        )

    @pl.when(steps > 0)
    def _():
        for copy in coming(0):
            copy.start()

    acc_s[...] = jnp.zeros_like(acc_s)
    probe_s[...] = jnp.zeros_like(probe_s)
    misfit_s[...] = jnp.zeros_like(misfit_s)
    lane = lax.broadcasted_iota(jnp.int32, (STRIP, LANES), 1)

    def step(n, carry):
        turn = n & 1

        @pl.when(n + 1 < steps)
        def _():
            for copy in coming(n + 1):
                copy.start()

        for copy in coming(n):
            copy.wait()
        entries = [list_ref[n * UNROLL + u] for u in range(UNROLL)]
        for u in range(UNROLL):
            slot = lax.shift_right_logical(entries[u], TILE_SHIFT)
            held = jnp.minimum(slot, slots - 1)
            misfit = jnp.zeros((STRIP, LANES), jnp.float32)
            for s in range(0, width, STRIP):
                fields = [
                    far_s[turn, u, pl.ds(h * width + s, STRIP), pl.ds(k * width, width)]
                    for k in range(modes)
                    for h in range(2)
                ]
                intensity = 1.0 + sum(f * f for f in fields)
                data = meas_ref[held, pl.ds(s, STRIP), :].astype(jnp.float32)
                inverse = lax.rsqrt(intensity)
                gap = intensity * inverse - data
                misfit = misfit + gap * gap
                factor = jnp.where(slot < slots, 1.0 - data * inverse, 0.0)
                for k in range(modes):
                    for h in range(2):
                        field_s[u, pl.ds(k * width + s, STRIP), pl.ds(h * width, width)] = (
                            fields[2 * k + h] * factor
                        ).astype(jnp.bfloat16)
            misfit_s[slot] = jnp.sum(misfit, axis=0, keepdims=True)
        for u in range(UNROLL):
            right_product(field_s, x_ref, half_s, u)
        for u in range(UNROLL):
            back_s[u] = jnp.dot(y_ref[...], half_s[u], preferred_element_type=jnp.float32)
        places = [window_of(entries[u], blocks) for u in range(UNROLL)]
        for s in range(0, width, STRIP):
            rows = pl.ds(s, STRIP)
            objs = [[patch_s[turn, u, a, rows, :].astype(jnp.float32) for a in range(2)] for u in range(UNROLL)]
            parts = [[None, None] for _ in range(UNROLL)]
            for k in range(modes):
                p_r = probe_ref[k, 0, rows, :]
                p_i = probe_ref[k, 1, rows, :]
                sum_r = probe_s[k, 0, rows, :]
                sum_i = probe_s[k, 1, rows, :]
                for u in range(UNROLL):
                    b_r = back_s[u, rows, pl.ds(k * width, width)]
                    b_i = back_s[u, pl.ds(width + s, STRIP), pl.ds(k * width, width)]
                    o_r, o_i = objs[u]
                    new_r = p_r * b_r + p_i * b_i
                    new_i = p_r * b_i - p_i * b_r
                    parts[u] = [new_r, new_i] if k == 0 else [parts[u][0] + new_r, parts[u][1] + new_i]
                    sum_r = sum_r + (o_r * b_r + o_i * b_i)
                    sum_i = sum_i + (o_r * b_i - o_i * b_r)
                probe_s[k, 0, rows, :] = sum_r
                probe_s[k, 1, rows, :] = sum_i
            for u in range(UNROLL):
                _, row, block, shift = places[u]
                keep = lane >= shift
                for a in range(2):
                    turned = pltpu.roll(parts[u][a], shift & (LANES - 1), 1)
                    spot = (a, block, pl.ds(row + s, STRIP), slice(None))
                    acc_s[spot] = acc_s[spot] + jnp.where(keep, turned, 0.0)
                    spot = (a, block + 1, pl.ds(row + s, STRIP), slice(None))
                    acc_s[spot] = acc_s[spot] + jnp.where(keep, 0.0, turned)
        return carry

    lax.fori_loop(0, steps, step, jnp.int32(0))
    groups = sums_ref.shape[0]
    rows = sums_ref.shape[1] - 8
    copies = [
        pltpu.make_async_copy(
            acc_s.at[a, b], grad_ref.at[a, :, pl.ds(b * LANES, LANES)], sems.at[a * blocks + b]
        )
        for a in range(2)
        for b in range(blocks)
    ]
    for copy in copies:
        copy.start()
    per_plane = width // rows
    for g in range(groups):
        plane, part = divmod(g, per_plane)
        sums_ref[g, pl.ds(0, rows), :] = probe_s[plane // 2, plane % 2, pl.ds(part * rows, rows), :]
        for s in range(CAP):
            sums_ref[g, pl.ds(rows + s, 1), :] = misfit_s[g * CAP + s]
        sums_ref[g, pl.ds(rows + CAP, 8 - CAP), :] = jnp.zeros((8 - CAP, LANES), jnp.float32)
    for copy in copies:
        copy.wait()


def receive_kernel(scale, pixels, slot_ref, sums_ref, probe_ref, misfit_ref):
    groups, rows = sums_ref.shape[0], probe_ref.shape[0]
    total = jnp.zeros((rows, LANES), jnp.float32)
    for g in range(groups):
        total = total + sums_ref[g, pl.ds(0, rows), :]
    probe_ref[...] = total * scale
    for i in range(slot_ref.shape[0]):
        slot = slot_ref[i]
        picked = sums_ref[lax.shift_right_logical(slot, 1), pl.ds(rows + (slot & 1), 1), :]
        misfit_ref[i] = jnp.sum(picked) * (1.0 / pixels)


SMEM = pl.BlockSpec(memory_space=pltpu.SMEM)
VMEM = pl.BlockSpec(memory_space=pltpu.VMEM)
ANY = pl.BlockSpec(memory_space=pl.ANY)


def kernels(tile_shape, modes, width, slots, per_device, groups):
    tile_width = tile_shape[-1]
    blocks = tile_width // LANES
    rows = modes * 2 * width // groups
    flops = slots // 2 * modes * 2 * (2 * width) ** 2 * width * 2
    staging = [
        pltpu.VMEM((2, UNROLL, 2 * width, modes * width), jnp.float32),
        pltpu.VMEM((2, UNROLL, 2, width, width), jnp.bfloat16),
        pltpu.VMEM((UNROLL, modes * width, 2 * width), jnp.bfloat16),
        pltpu.VMEM((UNROLL, 2 * width, modes * width), jnp.bfloat16),
    ]
    forward = pl.pallas_call(
        lambda *refs: forward_kernel(slots, *refs),
        out_shape=(
            jax.ShapeDtypeStruct((slots + UNROLL, 2 * width, modes * width), jnp.float32),
            jax.ShapeDtypeStruct((slots + UNROLL, 2, width, width), jnp.bfloat16),
        ),
        in_specs=[SMEM, ANY, VMEM, VMEM, VMEM],
        out_specs=(ANY, ANY),
        scratch_shapes=[
            pltpu.VMEM((2, blocks, tile_width, LANES), jnp.float32),
            *staging,
            pltpu.SemaphoreType.DMA((2 * blocks,)),
            pltpu.SemaphoreType.DMA((2, 2)),
        ],
        compiler_params=pltpu.CompilerParams(vmem_limit_bytes=48 << 20),
        cost_estimate=pl.CostEstimate(flops=flops, bytes_accessed=40_000_000, transcendentals=0),
        name="forward_windows",
    )
    backward = pl.pallas_call(
        lambda *refs: backward_kernel(slots, *refs),
        out_shape=(
            jax.ShapeDtypeStruct(tile_shape, jnp.float32),
            jax.ShapeDtypeStruct((groups, rows + 8, LANES), jnp.float32),
        ),
        in_specs=[SMEM, ANY, ANY, VMEM, VMEM, VMEM, VMEM],
        out_specs=(ANY, VMEM),
        scratch_shapes=[
            pltpu.VMEM((2, blocks, tile_width, LANES), jnp.float32),
            pltpu.VMEM((modes, 2, width, LANES), jnp.float32),
            pltpu.VMEM((slots + 1, 1, LANES), jnp.float32),
            *staging,
            pltpu.VMEM((UNROLL, 2 * width, modes * width), jnp.float32),
            pltpu.SemaphoreType.DMA((2 * blocks,)),
            pltpu.SemaphoreType.DMA((2, 2)),
        ],
        compiler_params=pltpu.CompilerParams(vmem_limit_bytes=48 << 20),
        cost_estimate=pl.CostEstimate(flops=flops, bytes_accessed=40_000_000, transcendentals=0),
        name="backward_windows",
    )
    return forward, backward


def local(obj, probe, measured, tile_of, inner):
    cols_along = lax.axis_size("ty")
    groups = lax.axis_size("tx") * cols_along
    depth = lax.axis_size("pos")
    modes, _, width, _ = probe.shape
    per_device = measured.shape[0]
    positions = per_device * groups * depth
    slots = groups * CAP
    plane = ("tx", "ty")
    my_tile = lax.axis_index("tx") * cols_along + lax.axis_index("ty")
    where = jnp.stack([my_tile, lax.axis_index("pos")]).astype(jnp.int32)
    packed = (tile_of[:, 0] << TILE_SHIFT) | (inner[:, 0] << ROW_BITS) | inner[:, 1]
    sizes = (groups, depth, per_device)

    outgoing, own_slots = pl.pallas_call(
        lambda *refs: send_kernel(*sizes, *refs),
        out_shape=(
            jax.ShapeDtypeStruct((slots, width, width), measured.dtype),
            jax.ShapeDtypeStruct((per_device,), jnp.int32),
        ),
        in_specs=[SMEM, SMEM, VMEM],
        out_specs=(VMEM, SMEM),
        name="send_slots",
    )(where, packed, measured)
    arrived = lax.all_to_all(
        outgoing.reshape(groups, CAP, width, width), plane, split_axis=0, concat_axis=0, tiled=True
    ).reshape(slots, width, width)
    listed = pl.pallas_call(
        lambda *refs: list_kernel(*sizes, *refs),
        out_shape=jax.ShapeDtypeStruct((slots + 2 * UNROLL + 4,), jnp.int32),
        in_specs=[SMEM, SMEM],
        out_specs=SMEM,
        cost_estimate=pl.CostEstimate(flops=1_000_000, bytes_accessed=10_000_000, transcendentals=0),
        name="list_windows",
    )(where, packed)
    tables = [jnp.asarray(table) for table in dft_blocks(width)]
    rows = modes * 2 * width // groups
    forward, backward = kernels(obj.shape, modes, width, slots, per_device, groups)
    far, patches = forward(listed, obj, probe, *tables)
    tile_grad, sums = backward(listed, far, patches, probe, arrived, *tables)
    shares = lax.psum_scatter(tile_grad, "pos", scatter_dimension=1, tiled=True)
    sums = lax.all_to_all(sums, plane, split_axis=0, concat_axis=0, tiled=True)
    probe_part, misfit = pl.pallas_call(
        lambda *refs: receive_kernel(1.0 / positions, width * width, *refs),
        out_shape=(
            jax.ShapeDtypeStruct((rows, LANES), jnp.float32),
            jax.ShapeDtypeStruct((per_device,), jnp.float32),
        ),
        in_specs=[SMEM, VMEM],
        out_specs=(VMEM, SMEM),
        name="receive_sums",
    )(own_slots, sums)
    hop = 1
    while hop < depth:
        partner = [(z, z ^ hop) for z in range(depth)]
        probe_part = probe_part + lax.ppermute(probe_part, "pos", partner)
        hop *= 2
    probe_total = lax.all_to_all(
        jnp.broadcast_to(probe_part, (groups, rows, LANES)), plane, split_axis=0, concat_axis=0, tiled=True
    )
    return (shares, probe_total.reshape(modes, 2, width, width), misfit)


def solution(mesh):
    return jax.shard_map(
        local,
        mesh=mesh,
        in_specs=(P(None, "tx", "ty"), P(), P(("tx", "ty", "pos"), None, None), P(), P()),
        out_specs=(P(None, ("tx", "pos"), "ty"), P(), P(("tx", "ty", "pos"))),
        check_vma=False,
    )
```

```python
import jax
import jax.numpy as jnp
import ml_dtypes
import numpy as np
from jax import lax
from jax.experimental import pallas as pl
from jax.experimental.pallas import tpu as pltpu
from jax.sharding import PartitionSpec as P

CAP = 2
UNROLL = 4
STRIP = 16
PACK = 32
LANES = 128
ROW_BITS = 10
TILE_SHIFT = 2 * ROW_BITS
LOW = (1 << ROW_BITS) - 1


def dft_blocks(width):
    counter = np.arange(width, dtype=np.int32)
    product = counter[:, None] * counter[None, :] % width
    angles = product.astype(np.float32) * np.float32(2.0 * np.pi / width)
    factor = np.float32(1.0) / np.sqrt(np.float32(width))
    c = (np.cos(angles) * factor).astype(ml_dtypes.bfloat16)
    s = (-np.sin(angles) * factor).astype(ml_dtypes.bfloat16)
    return np.block([[c, -s], [s, c]]), np.block([[c, s], [-s, c]])


def own_place(cols_along):
    return lax.axis_index("tx") * cols_along + lax.axis_index("ty"), lax.axis_index("pos")


def send_kernel(cols_along, depth, per_device, tile_ref, measured_ref, out_ref, slot_ref):
    tile, plane = own_place(cols_along)
    base = (tile * depth + plane) * per_device
    tiles = [tile_ref[base + i] for i in range(per_device)]
    for i in range(per_device):
        rank = jnp.int32(0)
        for j in range(i):
            rank = rank + (tiles[j] == tiles[i]).astype(jnp.int32)
        slot = tiles[i] * CAP + rank
        slot_ref[i] = slot
        out_ref[slot] = measured_ref[i]


def list_windows(cols_along, groups, depth, per_device, packed_ref, list_ref):
    tile, plane = own_place(cols_along)

    def one_group(group, count):
        base = (group * depth + plane) * per_device
        rank = jnp.int32(0)
        for i in range(per_device):
            value = packed_ref[base + i]
            hit = (lax.shift_right_logical(value, TILE_SHIFT) == tile).astype(jnp.int32)
            slot = group * CAP + rank
            list_ref[count] = (slot << TILE_SHIFT) | (value & ((1 << TILE_SHIFT) - 1))
            count = count + hit
            rank = rank + hit
        return count

    count = lax.fori_loop(0, groups, one_group, jnp.int32(0))
    for u in range(UNROLL - 1):
        list_ref[count + u] = jnp.int32((groups * CAP) << TILE_SHIFT)
    list_ref[groups * CAP + UNROLL] = (count + UNROLL - 1) // UNROLL


def window_of(entry, blocks):
    slot = lax.shift_right_logical(entry, TILE_SHIFT)
    row = lax.shift_right_logical(entry, ROW_BITS) & LOW
    col = entry & LOW
    block = jnp.minimum(lax.shift_right_logical(col, 7), blocks - 2)
    return slot, row, block, col - block * LANES


def patch_spot(width, part, row):
    return pl.ds(2 * width + part * PACK + row % PACK, STRIP), pl.ds(row // PACK * LANES, LANES)


def right_product(field_s, table_ref, half_s, u):
    width = LANES
    half = jnp.dot(field_s[u], table_ref[...], preferred_element_type=jnp.float32)
    for k in range(field_s.shape[1] // width):
        for h in range(2):
            half_s[u, pl.ds(h * width, width), pl.ds(k * width, width)] = half[
                k * width : (k + 1) * width, h * width : (h + 1) * width
            ].astype(jnp.bfloat16)


def forward_kernel(
    sizes,
    packed_ref,
    obj_ref,
    probe_ref,
    x_ref,
    y_ref,
    far_ref,
    list_ref,
    tile_s,
    far_s,
    field_s,
    half_s,
    sems,
    out_sems,
):
    width = LANES
    modes = probe_ref.shape[0]
    blocks = tile_s.shape[1]
    copies = [
        pltpu.make_async_copy(
            obj_ref.at[a, :, pl.ds(b * LANES, LANES)], tile_s.at[a, b], sems.at[a * blocks + b]
        )
        for a in range(2)
        for b in range(blocks)
    ]
    for copy in copies:
        copy.start()
    list_windows(*sizes, packed_ref, list_ref)
    steps = list_ref[sizes[1] * CAP + UNROLL]
    for copy in copies:
        copy.wait()

    def leaving(n):
        turn = n & 1
        there = pl.ds(n * UNROLL, UNROLL)
        return (
            pltpu.make_async_copy(far_s.at[turn], far_ref.at[there], out_sems.at[turn]),
        )

    lane = lax.broadcasted_iota(jnp.int32, (STRIP, LANES), 1)

    def step(n, carry):
        turn = n & 1

        @pl.when(n >= 2)
        def _():
            for copy in leaving(n - 2):
                copy.wait()

        places = [window_of(list_ref[n * UNROLL + u], blocks) for u in range(UNROLL)]
        for s in range(0, width, STRIP):
            objs = []
            for u in range(UNROLL):
                _, row, block, shift = places[u]
                back_shift = (LANES - shift) & (LANES - 1)
                own = lane < LANES - shift
                parts = []
                for a in range(2):
                    left = pltpu.roll(tile_s[a, block, pl.ds(row + s, STRIP), :], back_shift, 1)
                    right = pltpu.roll(tile_s[a, block + 1, pl.ds(row + s, STRIP), :], back_shift, 1)
                    rounded = jnp.where(own, left, right).astype(jnp.bfloat16)
                    patch = rounded.astype(jnp.float32)
                    far_s[(turn, u, *patch_spot(width, a, s))] = patch
                    parts.append(patch)
                objs.append(parts)
            for k in range(modes):
                p_r = probe_ref[k, 0, pl.ds(s, STRIP), :]
                p_i = probe_ref[k, 1, pl.ds(s, STRIP), :]
                for u in range(UNROLL):
                    o_r, o_i = objs[u]
                    at = pl.ds(k * width + s, STRIP)
                    field_s[u, at, pl.ds(0, width)] = (p_r * o_r - p_i * o_i).astype(jnp.bfloat16)
                    field_s[u, at, pl.ds(width, width)] = (p_r * o_i + p_i * o_r).astype(jnp.bfloat16)
        for u in range(UNROLL):
            right_product(field_s, y_ref, half_s, u)
        for u in range(UNROLL):
            far_s[turn, u, pl.ds(0, 2 * width), :] = jnp.dot(x_ref[...], half_s[u], preferred_element_type=jnp.float32)
        for copy in leaving(n):
            copy.start()
        return carry

    lax.fori_loop(0, steps, step, jnp.int32(0))
    for late in (2, 1):

        @pl.when(steps >= late)
        def _():
            for copy in leaving(steps - late):
                copy.wait()


def backward_kernel(
    slots,
    list_ref,
    far_ref,
    probe_ref,
    meas_ref,
    x_ref,
    y_ref,
    grad_ref,
    sums_ref,
    acc_s,
    probe_s,
    misfit_s,
    far_s,
    field_s,
    half_s,
    back_s,
    sems,
    in_sems,
):
    width = LANES
    modes = probe_ref.shape[0]
    blocks = acc_s.shape[1]
    steps = list_ref[slots + UNROLL]

    def coming(n):
        turn = n & 1
        there = pl.ds(n * UNROLL, UNROLL)
        return (
            pltpu.make_async_copy(far_ref.at[there], far_s.at[turn], in_sems.at[turn]),
        )

    @pl.when(steps > 0)
    def _():
        for copy in coming(0):
            copy.start()

    acc_s[...] = jnp.zeros_like(acc_s)
    probe_s[...] = jnp.zeros_like(probe_s)
    misfit_s[...] = jnp.zeros_like(misfit_s)
    lane = lax.broadcasted_iota(jnp.int32, (STRIP, LANES), 1)

    def step(n, carry):
        turn = n & 1

        @pl.when(n + 1 < steps)
        def _():
            for copy in coming(n + 1):
                copy.start()

        for copy in coming(n):
            copy.wait()
        entries = [list_ref[n * UNROLL + u] for u in range(UNROLL)]
        for u in range(UNROLL):
            slot = lax.shift_right_logical(entries[u], TILE_SHIFT)
            held = jnp.minimum(slot, slots - 1)
            misfit = jnp.zeros((STRIP, LANES), jnp.float32)
            for s in range(0, width, STRIP):
                fields = [
                    far_s[turn, u, pl.ds(h * width + s, STRIP), pl.ds(k * width, width)]
                    for k in range(modes)
                    for h in range(2)
                ]
                intensity = 1.0 + sum(f * f for f in fields)
                data = meas_ref[held, pl.ds(s, STRIP), :].astype(jnp.float32)
                inverse = lax.rsqrt(intensity)
                gap = intensity * inverse - data
                misfit = misfit + gap * gap
                factor = jnp.where(slot < slots, 1.0 - data * inverse, 0.0)
                for k in range(modes):
                    for h in range(2):
                        field_s[u, pl.ds(k * width + s, STRIP), pl.ds(h * width, width)] = (
                            fields[2 * k + h] * factor
                        ).astype(jnp.bfloat16)
            misfit_s[slot] = jnp.sum(misfit, axis=0, keepdims=True)
            right_product(field_s, x_ref, half_s, u)
            if u:
                back_s[u - 1] = jnp.dot(y_ref[...], half_s[u - 1], preferred_element_type=jnp.float32)
        back_s[UNROLL - 1] = jnp.dot(y_ref[...], half_s[UNROLL - 1], preferred_element_type=jnp.float32)
        places = [window_of(entries[u], blocks) for u in range(UNROLL)]
        for s in range(0, width, STRIP):
            rows = pl.ds(s, STRIP)
            objs = [[far_s[(turn, u, *patch_spot(width, a, s))] for a in range(2)] for u in range(UNROLL)]
            parts = [[None, None] for _ in range(UNROLL)]
            for k in range(modes):
                p_r = probe_ref[k, 0, rows, :]
                p_i = probe_ref[k, 1, rows, :]
                sum_r = probe_s[k, 0, rows, :]
                sum_i = probe_s[k, 1, rows, :]
                for u in range(UNROLL):
                    b_r = back_s[u, rows, pl.ds(k * width, width)]
                    b_i = back_s[u, pl.ds(width + s, STRIP), pl.ds(k * width, width)]
                    o_r, o_i = objs[u]
                    new_r = p_r * b_r + p_i * b_i
                    new_i = p_r * b_i - p_i * b_r
                    parts[u] = [new_r, new_i] if k == 0 else [parts[u][0] + new_r, parts[u][1] + new_i]
                    sum_r = sum_r + (o_r * b_r + o_i * b_i)
                    sum_i = sum_i + (o_r * b_i - o_i * b_r)
                probe_s[k, 0, rows, :] = sum_r
                probe_s[k, 1, rows, :] = sum_i
            for u in range(UNROLL):
                _, row, block, shift = places[u]
                keep = lane >= shift
                for a in range(2):
                    turned = pltpu.roll(parts[u][a], shift & (LANES - 1), 1)
                    spot = (a, block, pl.ds(row + s, STRIP), slice(None))
                    acc_s[spot] = acc_s[spot] + jnp.where(keep, turned, 0.0)
                    spot = (a, block + 1, pl.ds(row + s, STRIP), slice(None))
                    acc_s[spot] = acc_s[spot] + jnp.where(keep, 0.0, turned)
        return carry

    lax.fori_loop(0, steps, step, jnp.int32(0))
    groups = sums_ref.shape[0]
    rows = sums_ref.shape[1] - 8
    copies = [
        pltpu.make_async_copy(
            acc_s.at[a, b], grad_ref.at[a, :, pl.ds(b * LANES, LANES)], sems.at[a * blocks + b]
        )
        for a in range(2)
        for b in range(blocks)
    ]
    for copy in copies:
        copy.start()
    per_plane = width // rows
    for g in range(groups):
        plane, part = divmod(g, per_plane)
        sums_ref[g, pl.ds(0, rows), :] = probe_s[plane // 2, plane % 2, pl.ds(part * rows, rows), :]
        for s in range(CAP):
            sums_ref[g, pl.ds(rows + s, 1), :] = misfit_s[g * CAP + s]
        sums_ref[g, pl.ds(rows + CAP, 8 - CAP), :] = jnp.zeros((8 - CAP, LANES), jnp.float32)
    for copy in copies:
        copy.wait()


def receive_kernel(scale, pixels, slot_ref, sums_ref, probe_ref, misfit_ref):
    groups, rows = sums_ref.shape[0], probe_ref.shape[0]
    total = jnp.zeros((rows, LANES), jnp.float32)
    for g in range(groups):
        total = total + sums_ref[g, pl.ds(0, rows), :]
    probe_ref[...] = total * scale
    for i in range(slot_ref.shape[0]):
        slot = slot_ref[i]
        picked = sums_ref[lax.shift_right_logical(slot, 1), pl.ds(rows + (slot & 1), 1), :]
        misfit_ref[i] = jnp.sum(picked) * (1.0 / pixels)


SMEM = pl.BlockSpec(memory_space=pltpu.SMEM)
VMEM = pl.BlockSpec(memory_space=pltpu.VMEM)
ANY = pl.BlockSpec(memory_space=pl.ANY)


def kernels(tile_shape, modes, width, slots, per_device, groups, cols_along, depth):
    tile_width = tile_shape[-1]
    blocks = tile_width // LANES
    rows = modes * 2 * width // groups
    flops = slots // 2 * modes * 2 * (2 * width) ** 2 * width * 2
    staging = [
        pltpu.VMEM((2, UNROLL, 2 * width + 2 * PACK, modes * width), jnp.float32),
        pltpu.VMEM((UNROLL, modes * width, 2 * width), jnp.bfloat16),
        pltpu.VMEM((UNROLL, 2 * width, modes * width), jnp.bfloat16),
    ]
    forward = pl.pallas_call(
        lambda *refs: forward_kernel((cols_along, groups, depth, per_device), *refs),
        out_shape=(
            jax.ShapeDtypeStruct((slots + UNROLL, 2 * width + 2 * PACK, modes * width), jnp.float32),
            jax.ShapeDtypeStruct((slots + 2 * UNROLL + 4,), jnp.int32),
        ),
        in_specs=[SMEM, ANY, VMEM, VMEM, VMEM],
        out_specs=(ANY, SMEM),
        scratch_shapes=[
            pltpu.VMEM((2, blocks, tile_width, LANES), jnp.float32),
            *staging,
            pltpu.SemaphoreType.DMA((2 * blocks,)),
            pltpu.SemaphoreType.DMA((2,)),
        ],
        compiler_params=pltpu.CompilerParams(vmem_limit_bytes=48 << 20),
        cost_estimate=pl.CostEstimate(flops=flops, bytes_accessed=40_000_000, transcendentals=0),
        name="forward_windows",
    )
    backward = pl.pallas_call(
        lambda *refs: backward_kernel(slots, *refs),
        out_shape=(
            jax.ShapeDtypeStruct(tile_shape, jnp.float32),
            jax.ShapeDtypeStruct((groups, rows + 8, LANES), jnp.float32),
        ),
        in_specs=[SMEM, ANY, VMEM, VMEM, VMEM, VMEM],
        out_specs=(ANY, VMEM),
        scratch_shapes=[
            pltpu.VMEM((2, blocks, tile_width, LANES), jnp.float32),
            pltpu.VMEM((modes, 2, width, LANES), jnp.float32),
            pltpu.VMEM((slots + 1, 1, LANES), jnp.float32),
            *staging,
            pltpu.VMEM((UNROLL, 2 * width, modes * width), jnp.float32),
            pltpu.SemaphoreType.DMA((2 * blocks,)),
            pltpu.SemaphoreType.DMA((2,)),
        ],
        compiler_params=pltpu.CompilerParams(vmem_limit_bytes=48 << 20),
        cost_estimate=pl.CostEstimate(flops=flops, bytes_accessed=40_000_000, transcendentals=0),
        name="backward_windows",
    )
    return forward, backward


def local(obj, probe, measured, tile_of, inner):
    cols_along = lax.axis_size("ty")
    groups = lax.axis_size("tx") * cols_along
    depth = lax.axis_size("pos")
    modes, _, width, _ = probe.shape
    per_device = measured.shape[0]
    positions = per_device * groups * depth
    slots = groups * CAP
    plane = ("tx", "ty")
    outgoing, own_slots = pl.pallas_call(
        lambda *refs: send_kernel(cols_along, depth, per_device, *refs),
        out_shape=(
            jax.ShapeDtypeStruct((slots, width, width), measured.dtype),
            jax.ShapeDtypeStruct((per_device,), jnp.int32),
        ),
        in_specs=[SMEM, VMEM],
        out_specs=(VMEM, SMEM),
        name="send_slots",
    )(tile_of.reshape(positions), measured)
    arrived = lax.all_to_all(
        outgoing.reshape(groups, CAP, width, width), plane, split_axis=0, concat_axis=0, tiled=True
    ).reshape(slots, width, width)
    packed = (tile_of[:, 0] << TILE_SHIFT) | (inner[:, 0] << ROW_BITS) | inner[:, 1]
    tables = [jnp.asarray(table) for table in dft_blocks(width)]
    rows = modes * 2 * width // groups
    forward, backward = kernels(obj.shape, modes, width, slots, per_device, groups, cols_along, depth)
    far, listed = forward(packed, obj, probe, *tables)
    tile_grad, sums = backward(listed, far, probe, arrived, *tables)
    shares = lax.psum_scatter(tile_grad, "pos", scatter_dimension=1, tiled=True)
    sums = lax.all_to_all(sums, plane, split_axis=0, concat_axis=0, tiled=True)
    probe_part, misfit = pl.pallas_call(
        lambda *refs: receive_kernel(1.0 / positions, width * width, *refs),
        out_shape=(
            jax.ShapeDtypeStruct((rows, LANES), jnp.float32),
            jax.ShapeDtypeStruct((per_device,), jnp.float32),
        ),
        in_specs=[SMEM, VMEM],
        out_specs=(VMEM, SMEM),
        name="receive_sums",
    )(own_slots, sums)
    hop = 1
    while hop < depth:
        partner = [(z, z ^ hop) for z in range(depth)]
        probe_part = probe_part + lax.ppermute(probe_part, "pos", partner)
        hop *= 2
    probe_total = lax.all_to_all(
        jnp.broadcast_to(probe_part, (groups, rows, LANES)), plane, split_axis=0, concat_axis=0, tiled=True
    )
    return (shares, probe_total.reshape(modes, 2, width, width), misfit)


def solution(mesh):
    return jax.shard_map(
        local,
        mesh=mesh,
        in_specs=(P(None, "tx", "ty"), P(), P(("tx", "ty", "pos"), None, None), P(), P()),
        out_specs=(P(None, ("tx", "pos"), "ty"), P(), P(("tx", "ty", "pos"))),
        check_vma=False,
    )
```

```python
import jax
import jax.numpy as jnp
import ml_dtypes
import numpy as np
from jax import lax
from jax.experimental import pallas as pl
from jax.experimental.pallas import tpu as pltpu
from jax.sharding import PartitionSpec as P

CAP = 2
UNROLL = 4
STRIP = 16
PACK = 32
LANES = 128
ROW_BITS = 10
TILE_SHIFT = 2 * ROW_BITS
LOW = (1 << ROW_BITS) - 1


def dft_blocks(width):
    counter = np.arange(width, dtype=np.int32)
    product = counter[:, None] * counter[None, :] % width
    angles = product.astype(np.float32) * np.float32(2.0 * np.pi / width)
    factor = np.float32(1.0) / np.sqrt(np.float32(width))
    c = (np.cos(angles) * factor).astype(ml_dtypes.bfloat16)
    s = (-np.sin(angles) * factor).astype(ml_dtypes.bfloat16)
    return np.block([[c, -s], [s, c]]), np.block([[c, s], [-s, c]])


def own_place(cols_along):
    return lax.axis_index("tx") * cols_along + lax.axis_index("ty"), lax.axis_index("pos")


def send_kernel(cols_along, depth, per_device, tile_ref, measured_ref, out_ref, slot_ref):
    tile, plane = own_place(cols_along)
    base = (tile * depth + plane) * per_device
    tiles = [tile_ref[base + i] for i in range(per_device)]
    for i in range(per_device):
        rank = jnp.int32(0)
        for j in range(i):
            rank = rank + (tiles[j] == tiles[i]).astype(jnp.int32)
        slot = tiles[i] * CAP + rank
        slot_ref[i] = slot
        out_ref[slot] = measured_ref[i]


def list_windows(cols_along, groups, depth, per_device, packed_ref, list_ref):
    tile, plane = own_place(cols_along)

    def one_group(group, count):
        base = (group * depth + plane) * per_device
        values = [packed_ref[base + i] for i in range(per_device)]
        hits = [lax.shift_right_logical(value, TILE_SHIFT) == tile for value in values]
        first = last = jnp.int32(0)
        found = jnp.int32(0)
        for i in range(per_device):
            last = jnp.where(hits[i], values[i], last)
            first = jnp.where(hits[per_device - 1 - i], values[per_device - 1 - i], first)
            found = found + hits[i].astype(jnp.int32)
        for rank, value in enumerate((first, last)):
            list_ref[count + rank] = ((group * CAP + rank) << TILE_SHIFT) | (value & ((1 << TILE_SHIFT) - 1))
        return count + found

    count = lax.fori_loop(0, groups, one_group, jnp.int32(0))
    for u in range(UNROLL):
        list_ref[count + u] = jnp.int32((groups * CAP) << TILE_SHIFT)
    list_ref[groups * CAP + UNROLL] = (count + UNROLL - 1) // UNROLL


def window_of(entry, blocks):
    slot = lax.shift_right_logical(entry, TILE_SHIFT)
    row = lax.shift_right_logical(entry, ROW_BITS) & LOW
    col = entry & LOW
    block = jnp.minimum(lax.shift_right_logical(col, 7), blocks - 2)
    return slot, row, block, col - block * LANES


def patch_spot(width, part, row):
    return pl.ds(2 * width + part * PACK + row % PACK, STRIP), pl.ds(row // PACK * LANES, LANES)


def right_product(field_s, table_ref, half_s, u):
    width = LANES
    half = jnp.dot(field_s[u], table_ref[...], preferred_element_type=jnp.float32)
    for k in range(field_s.shape[1] // width):
        for h in range(2):
            half_s[u, pl.ds(h * width, width), pl.ds(k * width, width)] = half[
                k * width : (k + 1) * width, h * width : (h + 1) * width
            ].astype(jnp.bfloat16)


def forward_kernel(
    sizes,
    packed_ref,
    obj_ref,
    probe_ref,
    x_ref,
    y_ref,
    far_ref,
    list_ref,
    tile_s,
    far_s,
    field_s,
    half_s,
    sems,
    out_sems,
):
    width = LANES
    modes = probe_ref.shape[0]
    blocks = tile_s.shape[1]
    copies = [
        pltpu.make_async_copy(
            obj_ref.at[a, :, pl.ds(b * LANES, LANES)], tile_s.at[a, b], sems.at[a * blocks + b]
        )
        for a in range(2)
        for b in range(blocks)
    ]
    for copy in copies:
        copy.start()
    list_windows(*sizes, packed_ref, list_ref)
    steps = list_ref[sizes[1] * CAP + UNROLL]
    for copy in copies:
        copy.wait()

    def leaving(n):
        turn = n & 1
        there = pl.ds(n * UNROLL, UNROLL)
        return (
            pltpu.make_async_copy(far_s.at[turn], far_ref.at[there], out_sems.at[turn]),
        )

    lane = lax.broadcasted_iota(jnp.int32, (STRIP, LANES), 1)

    def step(n, carry):
        turn = n & 1

        @pl.when(n >= 2)
        def _():
            for copy in leaving(n - 2):
                copy.wait()

        places = [window_of(list_ref[n * UNROLL + u], blocks) for u in range(UNROLL)]
        for s in range(0, width, STRIP):
            objs = []
            for u in range(UNROLL):
                _, row, block, shift = places[u]
                back_shift = (LANES - shift) & (LANES - 1)
                own = lane < LANES - shift
                parts = []
                for a in range(2):
                    left = pltpu.roll(tile_s[a, block, pl.ds(row + s, STRIP), :], back_shift, 1)
                    right = pltpu.roll(tile_s[a, block + 1, pl.ds(row + s, STRIP), :], back_shift, 1)
                    rounded = jnp.where(own, left, right).astype(jnp.bfloat16)
                    patch = rounded.astype(jnp.float32)
                    far_s[(turn, u, *patch_spot(width, a, s))] = patch
                    parts.append(patch)
                objs.append(parts)
            for k in range(modes):
                p_r = probe_ref[k, 0, pl.ds(s, STRIP), :]
                p_i = probe_ref[k, 1, pl.ds(s, STRIP), :]
                for u in range(UNROLL):
                    o_r, o_i = objs[u]
                    at = pl.ds(k * width + s, STRIP)
                    field_s[u, at, pl.ds(0, width)] = (p_r * o_r - p_i * o_i).astype(jnp.bfloat16)
                    field_s[u, at, pl.ds(width, width)] = (p_r * o_i + p_i * o_r).astype(jnp.bfloat16)
        for u in range(UNROLL):
            right_product(field_s, y_ref, half_s, u)
        for u in range(UNROLL):
            far_s[turn, u, pl.ds(0, 2 * width), :] = jnp.dot(x_ref[...], half_s[u], preferred_element_type=jnp.float32)
        for copy in leaving(n):
            copy.start()
        return carry

    lax.fori_loop(0, steps, step, jnp.int32(0))
    for late in (2, 1):

        @pl.when(steps >= late)
        def _():
            for copy in leaving(steps - late):
                copy.wait()


def backward_kernel(
    slots,
    list_ref,
    far_ref,
    probe_ref,
    meas_ref,
    x_ref,
    y_ref,
    grad_ref,
    sums_ref,
    acc_s,
    probe_s,
    misfit_s,
    far_s,
    field_s,
    half_s,
    back_s,
    sems,
    in_sems,
):
    width = LANES
    modes = probe_ref.shape[0]
    blocks = acc_s.shape[1]
    steps = list_ref[slots + UNROLL]

    def coming(n):
        turn = lax.rem(n, 3)
        there = pl.ds(n * UNROLL, UNROLL)
        return pltpu.make_async_copy(far_ref.at[there], far_s.at[turn], in_sems.at[turn])

    @pl.when(steps > 0)
    def _():
        coming(0).start()

    acc_s[...] = jnp.zeros_like(acc_s)
    probe_s[...] = jnp.zeros_like(probe_s)
    misfit_s[...] = jnp.zeros_like(misfit_s)
    early, late = range(UNROLL // 2), range(UNROLL // 2, UNROLL)
    for u in late:
        back_s[u] = jnp.zeros(back_s.shape[1:], jnp.float32)
        far_s[2, u, pl.ds(2 * width, 2 * PACK), :] = jnp.zeros((2 * PACK, modes * width), jnp.float32)
    lane = lax.broadcasted_iota(jnp.int32, (STRIP, LANES), 1)

    def first_product(turn, u, entry):
        slot = lax.shift_right_logical(entry, TILE_SHIFT)
        held = jnp.minimum(slot, slots - 1)
        misfit = jnp.zeros((STRIP, LANES), jnp.float32)
        for s in range(0, width, STRIP):
            fields = [
                far_s[turn, u, pl.ds(h * width + s, STRIP), pl.ds(k * width, width)]
                for k in range(modes)
                for h in range(2)
            ]
            intensity = 1.0 + sum(f * f for f in fields)
            data = meas_ref[held, pl.ds(s, STRIP), :].astype(jnp.float32)
            inverse = lax.rsqrt(intensity)
            gap = intensity * inverse - data
            misfit = misfit + gap * gap
            factor = jnp.where(slot < slots, 1.0 - data * inverse, 0.0)
            for k in range(modes):
                for h in range(2):
                    field_s[u, pl.ds(k * width + s, STRIP), pl.ds(h * width, width)] = (
                        fields[2 * k + h] * factor
                    ).astype(jnp.bfloat16)
        misfit_s[slot] = jnp.sum(misfit, axis=0, keepdims=True)
        right_product(field_s, x_ref, half_s, u)

    def second_product(u):
        back_s[u] = jnp.dot(y_ref[...], half_s[u], preferred_element_type=jnp.float32)

    def add_strips(turn, members, entries, strips):
        places = [window_of(entry, blocks) for entry in entries]
        count = len(entries)
        for s in strips:
            rows = pl.ds(s, STRIP)
            objs = [[far_s[(turn, u, *patch_spot(width, a, s))] for a in range(2)] for u in members]
            parts = [None] * count
            for k in range(modes):
                p_r = probe_ref[k, 0, rows, :]
                p_i = probe_ref[k, 1, rows, :]
                sum_r = probe_s[k, 0, rows, :]
                sum_i = probe_s[k, 1, rows, :]
                for n, u in enumerate(members):
                    b_r = back_s[u, rows, pl.ds(k * width, width)]
                    b_i = back_s[u, pl.ds(width + s, STRIP), pl.ds(k * width, width)]
                    o_r, o_i = objs[n]
                    new_r = p_r * b_r + p_i * b_i
                    new_i = p_r * b_i - p_i * b_r
                    parts[n] = [new_r, new_i] if k == 0 else [parts[n][0] + new_r, parts[n][1] + new_i]
                    sum_r = sum_r + (o_r * b_r + o_i * b_i)
                    sum_i = sum_i + (o_r * b_i - o_i * b_r)
                probe_s[k, 0, rows, :] = sum_r
                probe_s[k, 1, rows, :] = sum_i
            for n in range(count):
                _, row, block, shift = places[n]
                keep = lane >= shift
                for a in range(2):
                    turned = pltpu.roll(parts[n][a], shift & (LANES - 1), 1)
                    spot = (a, block, pl.ds(row + s, STRIP), slice(None))
                    acc_s[spot] = acc_s[spot] + jnp.where(keep, turned, 0.0)
                    spot = (a, block + 1, pl.ds(row + s, STRIP), slice(None))
                    acc_s[spot] = acc_s[spot] + jnp.where(keep, 0.0, turned)

    half_way = width // 2
    upper, lower = range(0, half_way, STRIP), range(half_way, width, STRIP)

    def products_beside(turn, members, entries, sums):
        first_product(turn, members[0], entries[0])
        add_strips(*sums, upper)
        for at in range(1, len(members)):
            first_product(turn, members[at], entries[at])
            second_product(members[at - 1])
        add_strips(*sums, lower)
        second_product(members[-1])

    def entries_of(n, members):
        return [list_ref[jnp.maximum(n, 0) * UNROLL + u] for u in members]

    def step(n, carry):
        turn = lax.rem(n, 3)

        @pl.when(n + 1 < steps)
        def _():
            coming(n + 1).start()

        coming(n).wait()
        now = entries_of(n, early)
        products_beside(turn, early, now, (lax.rem(n + 2, 3), late, entries_of(n - 1, late)))
        products_beside(turn, late, entries_of(n, late), (turn, early, now))
        return carry

    lax.fori_loop(0, steps, step, jnp.int32(0))
    add_strips(lax.rem(steps + 2, 3), late, entries_of(steps - 1, late), range(0, width, STRIP))
    groups = sums_ref.shape[0]
    rows = sums_ref.shape[1] - 8
    copies = [
        pltpu.make_async_copy(
            acc_s.at[a, b], grad_ref.at[a, :, pl.ds(b * LANES, LANES)], sems.at[a * blocks + b]
        )
        for a in range(2)
        for b in range(blocks)
    ]
    for copy in copies:
        copy.start()
    per_plane = width // rows
    for g in range(groups):
        plane, part = divmod(g, per_plane)
        sums_ref[g, pl.ds(0, rows), :] = probe_s[plane // 2, plane % 2, pl.ds(part * rows, rows), :]
        for s in range(CAP):
            sums_ref[g, pl.ds(rows + s, 1), :] = misfit_s[g * CAP + s]
        sums_ref[g, pl.ds(rows + CAP, 8 - CAP), :] = jnp.zeros((8 - CAP, LANES), jnp.float32)
    for copy in copies:
        copy.wait()


def receive_kernel(scale, pixels, slot_ref, sums_ref, probe_ref, misfit_ref):
    groups, rows = sums_ref.shape[0], probe_ref.shape[0]
    total = jnp.zeros((rows, LANES), jnp.float32)
    for g in range(groups):
        total = total + sums_ref[g, pl.ds(0, rows), :]
    probe_ref[...] = total * scale
    for i in range(slot_ref.shape[0]):
        slot = slot_ref[i]
        picked = sums_ref[lax.shift_right_logical(slot, 1), pl.ds(rows + (slot & 1), 1), :]
        misfit_ref[i] = jnp.sum(picked) * (1.0 / pixels)


SMEM = pl.BlockSpec(memory_space=pltpu.SMEM)
VMEM = pl.BlockSpec(memory_space=pltpu.VMEM)
ANY = pl.BlockSpec(memory_space=pl.ANY)


def kernels(tile_shape, modes, width, slots, per_device, groups, cols_along, depth):
    tile_width = tile_shape[-1]
    blocks = tile_width // LANES
    rows = modes * 2 * width // groups
    flops = slots // 2 * modes * 2 * (2 * width) ** 2 * width * 2
    far_buffers = [
        pltpu.VMEM((turns, UNROLL, 2 * width + 2 * PACK, modes * width), jnp.float32) for turns in (2, 3)
    ]
    staging = [
        pltpu.VMEM((UNROLL, modes * width, 2 * width), jnp.bfloat16),
        pltpu.VMEM((UNROLL, 2 * width, modes * width), jnp.bfloat16),
    ]
    forward = pl.pallas_call(
        lambda *refs: forward_kernel((cols_along, groups, depth, per_device), *refs),
        out_shape=(
            jax.ShapeDtypeStruct((slots + UNROLL, 2 * width + 2 * PACK, modes * width), jnp.float32),
            jax.ShapeDtypeStruct((slots + 2 * UNROLL + 4,), jnp.int32),
        ),
        in_specs=[SMEM, ANY, VMEM, VMEM, VMEM],
        out_specs=(ANY, SMEM),
        scratch_shapes=[
            pltpu.VMEM((2, blocks, tile_width, LANES), jnp.float32),
            far_buffers[0],
            *staging,
            pltpu.SemaphoreType.DMA((2 * blocks,)),
            pltpu.SemaphoreType.DMA((2,)),
        ],
        compiler_params=pltpu.CompilerParams(vmem_limit_bytes=55 << 20),
        cost_estimate=pl.CostEstimate(flops=flops, bytes_accessed=40_000_000, transcendentals=0),
        name="forward_windows",
    )
    backward = pl.pallas_call(
        lambda *refs: backward_kernel(slots, *refs),
        out_shape=(
            jax.ShapeDtypeStruct(tile_shape, jnp.float32),
            jax.ShapeDtypeStruct((groups, rows + 8, LANES), jnp.float32),
        ),
        in_specs=[SMEM, ANY, VMEM, VMEM, VMEM, VMEM],
        out_specs=(ANY, VMEM),
        scratch_shapes=[
            pltpu.VMEM((2, blocks, tile_width, LANES), jnp.float32),
            pltpu.VMEM((modes, 2, width, LANES), jnp.float32),
            pltpu.VMEM((slots + 1, 1, LANES), jnp.float32),
            far_buffers[1],
            *staging,
            pltpu.VMEM((UNROLL, 2 * width, modes * width), jnp.float32),
            pltpu.SemaphoreType.DMA((2 * blocks,)),
            pltpu.SemaphoreType.DMA((3,)),
        ],
        compiler_params=pltpu.CompilerParams(vmem_limit_bytes=48 << 20),
        cost_estimate=pl.CostEstimate(flops=flops, bytes_accessed=40_000_000, transcendentals=0),
        name="backward_windows",
    )
    return forward, backward


def local(obj, probe, measured, tile_of, inner):
    cols_along = lax.axis_size("ty")
    groups = lax.axis_size("tx") * cols_along
    depth = lax.axis_size("pos")
    modes, _, width, _ = probe.shape
    per_device = measured.shape[0]
    positions = per_device * groups * depth
    slots = groups * CAP
    plane = ("tx", "ty")
    outgoing, own_slots = pl.pallas_call(
        lambda *refs: send_kernel(cols_along, depth, per_device, *refs),
        out_shape=(
            jax.ShapeDtypeStruct((slots, width, width), measured.dtype),
            jax.ShapeDtypeStruct((per_device,), jnp.int32),
        ),
        in_specs=[SMEM, VMEM],
        out_specs=(VMEM, SMEM),
        name="send_slots",
    )(tile_of.reshape(positions), measured)
    arrived = lax.all_to_all(
        outgoing.reshape(groups, CAP, width, width), plane, split_axis=0, concat_axis=0, tiled=True
    ).reshape(slots, width, width)
    packed = (tile_of[:, 0] << TILE_SHIFT) | (inner[:, 0] << ROW_BITS) | inner[:, 1]
    tables = [jnp.asarray(table) for table in dft_blocks(width)]
    rows = modes * 2 * width // groups
    forward, backward = kernels(obj.shape, modes, width, slots, per_device, groups, cols_along, depth)
    far, listed = forward(packed, obj, probe, *tables)
    tile_grad, sums = backward(listed, far, probe, arrived, *tables)
    shares = lax.psum_scatter(tile_grad, "pos", scatter_dimension=1, tiled=True)
    sums = lax.all_to_all(sums, plane, split_axis=0, concat_axis=0, tiled=True)
    probe_part, misfit = pl.pallas_call(
        lambda *refs: receive_kernel(1.0 / positions, width * width, *refs),
        out_shape=(
            jax.ShapeDtypeStruct((rows, LANES), jnp.float32),
            jax.ShapeDtypeStruct((per_device,), jnp.float32),
        ),
        in_specs=[SMEM, VMEM],
        out_specs=(VMEM, SMEM),
        name="receive_sums",
    )(own_slots, sums)
    hop = 1
    while hop < depth:
        partner = [(z, z ^ hop) for z in range(depth)]
        probe_part = probe_part + lax.ppermute(probe_part, "pos", partner)
        hop *= 2
    probe_total = lax.all_to_all(
        jnp.broadcast_to(probe_part, (groups, rows, LANES)), plane, split_axis=0, concat_axis=0, tiled=True
    )
    return (shares, probe_total.reshape(modes, 2, width, width), misfit)


def solution(mesh):
    return jax.shard_map(
        local,
        mesh=mesh,
        in_specs=(P(None, "tx", "ty"), P(), P(("tx", "ty", "pos"), None, None), P(), P()),
        out_specs=(P(None, ("tx", "pos"), "ty"), P(), P(("tx", "ty", "pos"))),
        check_vma=False,
    )
```

```python
import jax
import jax.numpy as jnp
import ml_dtypes
import numpy as np
from jax import lax
from jax.experimental import pallas as pl
from jax.experimental.pallas import tpu as pltpu
from jax.sharding import PartitionSpec as P

CAP = 2
UNROLL = 4
STRIP = 16
PACK = 32
LANES = 128
ROW_BITS = 10
TILE_SHIFT = 2 * ROW_BITS
LOW = (1 << ROW_BITS) - 1


def dft_blocks(width):
    counter = np.arange(width, dtype=np.int32)
    product = counter[:, None] * counter[None, :] % width
    angles = product.astype(np.float32) * np.float32(2.0 * np.pi / width)
    factor = np.float32(1.0) / np.sqrt(np.float32(width))
    c = (np.cos(angles) * factor).astype(ml_dtypes.bfloat16)
    s = (-np.sin(angles) * factor).astype(ml_dtypes.bfloat16)
    return np.block([[c, -s], [s, c]]), np.block([[c, s], [-s, c]])


def own_place(cols_along):
    return lax.axis_index("tx") * cols_along + lax.axis_index("ty"), lax.axis_index("pos")


def send_kernel(cols_along, depth, per_device, tile_ref, measured_ref, out_ref, slot_ref):
    tile, plane = own_place(cols_along)
    base = (tile * depth + plane) * per_device
    tiles = [tile_ref[base + i] for i in range(per_device)]
    for i in range(per_device):
        rank = jnp.int32(0)
        for j in range(i):
            rank = rank + (tiles[j] == tiles[i]).astype(jnp.int32)
        slot = tiles[i] * CAP + rank
        slot_ref[i] = slot
        out_ref[slot] = measured_ref[i]


def list_windows(cols_along, groups, depth, per_device, packed_ref, list_ref):
    tile, plane = own_place(cols_along)

    def one_group(group, count):
        base = (group * depth + plane) * per_device
        values = [packed_ref[base + i] for i in range(per_device)]
        hits = [lax.shift_right_logical(value, TILE_SHIFT) == tile for value in values]
        first = last = jnp.int32(0)
        found = jnp.int32(0)
        for i in range(per_device):
            last = jnp.where(hits[i], values[i], last)
            first = jnp.where(hits[per_device - 1 - i], values[per_device - 1 - i], first)
            found = found + hits[i].astype(jnp.int32)
        for rank, value in enumerate((first, last)):
            list_ref[count + rank] = ((group * CAP + rank) << TILE_SHIFT) | (value & ((1 << TILE_SHIFT) - 1))
        return count + found

    count = lax.fori_loop(0, groups, one_group, jnp.int32(0))
    for u in range(UNROLL):
        list_ref[count + u] = jnp.int32((groups * CAP) << TILE_SHIFT)
    list_ref[groups * CAP + UNROLL] = (count + UNROLL - 1) // UNROLL


def window_of(entry, blocks):
    slot = lax.shift_right_logical(entry, TILE_SHIFT)
    row = lax.shift_right_logical(entry, ROW_BITS) & LOW
    col = entry & LOW
    block = jnp.minimum(lax.shift_right_logical(col, 7), blocks - 2)
    return slot, row, block, col - block * LANES


def patch_spot(width, part, row):
    return pl.ds(2 * width + part * PACK + row % PACK, STRIP), pl.ds(row // PACK * LANES, LANES)


def right_product(field_s, table_ref, half_ref, u):
    width = LANES
    half = jnp.dot(field_s[u], table_ref[...], preferred_element_type=jnp.float32)
    for k in range(field_s.shape[1] // width):
        for h in range(2):
            half_ref[pl.ds(h * width, width), pl.ds(k * width, width)] = half[
                k * width : (k + 1) * width, h * width : (h + 1) * width
            ].astype(jnp.bfloat16)


def forward_kernel(
    sizes,
    packed_ref,
    obj_ref,
    probe_ref,
    y_ref,
    kept_ref,
    list_ref,
    tile_s,
    kept_s,
    field_s,
    sems,
    out_sems,
):
    width = LANES
    modes = probe_ref.shape[0]
    blocks = tile_s.shape[1]
    copies = [
        pltpu.make_async_copy(
            obj_ref.at[a, :, pl.ds(b * LANES, LANES)], tile_s.at[a, b], sems.at[a * blocks + b]
        )
        for a in range(2)
        for b in range(blocks)
    ]
    for copy in copies:
        copy.start()
    list_windows(*sizes, packed_ref, list_ref)
    steps = list_ref[sizes[1] * CAP + UNROLL]
    for copy in copies:
        copy.wait()

    def leaving(n):
        turn = n & 1
        return [
            pltpu.make_async_copy(kept_s.at[turn, u], kept_ref.at[n * UNROLL + u], out_sems.at[turn, u])
            for u in range(UNROLL)
        ]

    lane = lax.broadcasted_iota(jnp.int32, (STRIP, LANES), 1)

    def step(n, carry):
        turn = n & 1

        @pl.when(n >= 2)
        def _():
            for copy in leaving(n - 2):
                copy.wait()

        places = [window_of(list_ref[n * UNROLL + u], blocks) for u in range(UNROLL)]
        for s in range(0, width, STRIP):
            objs = []
            for u in range(UNROLL):
                _, row, block, shift = places[u]
                back_shift = (LANES - shift) & (LANES - 1)
                own = lane < LANES - shift
                parts = []
                for a in range(2):
                    left = pltpu.roll(tile_s[a, block, pl.ds(row + s, STRIP), :], back_shift, 1)
                    right = pltpu.roll(tile_s[a, block + 1, pl.ds(row + s, STRIP), :], back_shift, 1)
                    rounded = jnp.where(own, left, right).astype(jnp.bfloat16)
                    kept_s[(turn, u, *patch_spot(width, a, s))] = rounded
                    parts.append(rounded.astype(jnp.float32))
                objs.append(parts)
            for k in range(modes):
                p_r = probe_ref[k, 0, pl.ds(s, STRIP), :]
                p_i = probe_ref[k, 1, pl.ds(s, STRIP), :]
                for u in range(UNROLL):
                    o_r, o_i = objs[u]
                    at = pl.ds(k * width + s, STRIP)
                    field_s[u, at, pl.ds(0, width)] = (p_r * o_r - p_i * o_i).astype(jnp.bfloat16)
                    field_s[u, at, pl.ds(width, width)] = (p_r * o_i + p_i * o_r).astype(jnp.bfloat16)
        for u in range(UNROLL):
            right_product(field_s, y_ref, kept_s.at[turn, u], u)
        for copy in leaving(n):
            copy.start()
        return carry

    lax.fori_loop(0, steps, step, jnp.int32(0))
    for late in (2, 1):

        @pl.when(steps >= late)
        def _():
            for copy in leaving(steps - late):
                copy.wait()


def backward_kernel(
    slots,
    list_ref,
    kept_ref,
    probe_ref,
    meas_ref,
    x_ref,
    y_ref,
    grad_ref,
    sums_ref,
    acc_s,
    probe_s,
    misfit_s,
    kept_s,
    field_s,
    half_s,
    far_s,
    back_s,
    sems,
    in_sems,
):
    width = LANES
    modes = probe_ref.shape[0]
    blocks = acc_s.shape[1]
    steps = list_ref[slots + UNROLL]

    def coming(n):
        turn = lax.rem(n, 3)
        return [
            pltpu.make_async_copy(kept_ref.at[n * UNROLL + u], kept_s.at[turn, u], in_sems.at[turn, u])
            for u in range(UNROLL)
        ]

    @pl.when(steps > 0)
    def _():
        for copy in coming(0):
            copy.start()

    acc_s[...] = jnp.zeros_like(acc_s)
    probe_s[...] = jnp.zeros_like(probe_s)
    misfit_s[...] = jnp.zeros_like(misfit_s)
    early, late = range(UNROLL // 2), range(UNROLL // 2, UNROLL)
    for u in late:
        back_s[u] = jnp.zeros(back_s.shape[1:], jnp.float32)
        kept_s[2, u, pl.ds(2 * width, 2 * PACK), :] = jnp.zeros((2 * PACK, modes * width), jnp.bfloat16)
    lane = lax.broadcasted_iota(jnp.int32, (STRIP, LANES), 1)

    def far_field(turn, u):
        far_s[u] = jnp.dot(x_ref[...], kept_s[turn, u, pl.ds(0, 2 * width), :], preferred_element_type=jnp.float32)

    def first_product(u, entry):
        slot = lax.shift_right_logical(entry, TILE_SHIFT)
        held = jnp.minimum(slot, slots - 1)
        misfit = jnp.zeros((STRIP, LANES), jnp.float32)
        for s in range(0, width, STRIP):
            fields = [
                far_s[u, pl.ds(h * width + s, STRIP), pl.ds(k * width, width)]
                for k in range(modes)
                for h in range(2)
            ]
            intensity = 1.0 + sum(f * f for f in fields)
            data = meas_ref[held, pl.ds(s, STRIP), :].astype(jnp.float32)
            inverse = lax.rsqrt(intensity)
            gap = intensity * inverse - data
            misfit = misfit + gap * gap
            factor = jnp.where(slot < slots, 1.0 - data * inverse, 0.0)
            for k in range(modes):
                for h in range(2):
                    field_s[u, pl.ds(k * width + s, STRIP), pl.ds(h * width, width)] = (
                        fields[2 * k + h] * factor
                    ).astype(jnp.bfloat16)
        misfit_s[slot] = jnp.sum(misfit, axis=0, keepdims=True)
        right_product(field_s, x_ref, half_s.at[u], u)

    def second_product(u):
        back_s[u] = jnp.dot(y_ref[...], half_s[u], preferred_element_type=jnp.float32)

    def add_strips(turn, members, entries, strips):
        places = [window_of(entry, blocks) for entry in entries]
        count = len(entries)
        for s in strips:
            rows = pl.ds(s, STRIP)
            objs = [
                [kept_s[(turn, u, *patch_spot(width, a, s))].astype(jnp.float32) for a in range(2)] for u in members
            ]
            parts = [None] * count
            for k in range(modes):
                p_r = probe_ref[k, 0, rows, :]
                p_i = probe_ref[k, 1, rows, :]
                sum_r = probe_s[k, 0, rows, :]
                sum_i = probe_s[k, 1, rows, :]
                for n, u in enumerate(members):
                    b_r = back_s[u, rows, pl.ds(k * width, width)]
                    b_i = back_s[u, pl.ds(width + s, STRIP), pl.ds(k * width, width)]
                    o_r, o_i = objs[n]
                    new_r = p_r * b_r + p_i * b_i
                    new_i = p_r * b_i - p_i * b_r
                    parts[n] = [new_r, new_i] if k == 0 else [parts[n][0] + new_r, parts[n][1] + new_i]
                    sum_r = sum_r + (o_r * b_r + o_i * b_i)
                    sum_i = sum_i + (o_r * b_i - o_i * b_r)
                probe_s[k, 0, rows, :] = sum_r
                probe_s[k, 1, rows, :] = sum_i
            for n in range(count):
                _, row, block, shift = places[n]
                keep = lane >= shift
                for a in range(2):
                    turned = pltpu.roll(parts[n][a], shift & (LANES - 1), 1)
                    spot = (a, block, pl.ds(row + s, STRIP), slice(None))
                    acc_s[spot] = acc_s[spot] + jnp.where(keep, turned, 0.0)
                    spot = (a, block + 1, pl.ds(row + s, STRIP), slice(None))
                    acc_s[spot] = acc_s[spot] + jnp.where(keep, 0.0, turned)

    half_way = width // 2
    upper, lower = range(0, half_way, STRIP), range(half_way, width, STRIP)

    def products_beside(turn, members, entries, sums, ahead):
        first_product(members[0], entries[0])
        for u in ahead:
            far_field(turn, u)
        add_strips(*sums, upper)
        for at in range(1, len(members)):
            first_product(members[at], entries[at])
            second_product(members[at - 1])
        add_strips(*sums, lower)
        second_product(members[-1])

    def entries_of(n, members):
        return [list_ref[jnp.maximum(n, 0) * UNROLL + u] for u in members]

    def step(n, carry):
        turn = lax.rem(n, 3)

        @pl.when(n + 1 < steps)
        def _():
            for copy in coming(n + 1):
                copy.start()

        for copy in coming(n):
            copy.wait()
        now = entries_of(n, early)
        for u in early:
            far_field(turn, u)
        products_beside(turn, early, now, (lax.rem(n + 2, 3), late, entries_of(n - 1, late)), late)
        products_beside(turn, late, entries_of(n, late), (turn, early, now), ())
        return carry

    lax.fori_loop(0, steps, step, jnp.int32(0))
    add_strips(lax.rem(steps + 2, 3), late, entries_of(steps - 1, late), range(0, width, STRIP))
    groups = sums_ref.shape[0]
    rows = sums_ref.shape[1] - 8
    copies = [
        pltpu.make_async_copy(
            acc_s.at[a, b], grad_ref.at[a, :, pl.ds(b * LANES, LANES)], sems.at[a * blocks + b]
        )
        for a in range(2)
        for b in range(blocks)
    ]
    for copy in copies:
        copy.start()
    per_plane = width // rows
    for g in range(groups):
        plane, part = divmod(g, per_plane)
        sums_ref[g, pl.ds(0, rows), :] = probe_s[plane // 2, plane % 2, pl.ds(part * rows, rows), :]
        for s in range(CAP):
            sums_ref[g, pl.ds(rows + s, 1), :] = misfit_s[g * CAP + s]
        sums_ref[g, pl.ds(rows + CAP, 8 - CAP), :] = jnp.zeros((8 - CAP, LANES), jnp.float32)
    for copy in copies:
        copy.wait()


def receive_kernel(pixels, slot_ref, sums_ref, probe_ref, misfit_ref):
    groups, rows = sums_ref.shape[0], probe_ref.shape[0]
    total = jnp.zeros((rows, LANES), jnp.float32)
    for g in range(groups):
        total = total + sums_ref[g, pl.ds(0, rows), :]
    probe_ref[...] = total
    for i in range(slot_ref.shape[0]):
        slot = slot_ref[i]
        picked = sums_ref[lax.shift_right_logical(slot, 1), pl.ds(rows + (slot & 1), 1), :]
        misfit_ref[i] = jnp.sum(picked) * (1.0 / pixels)


SMEM = pl.BlockSpec(memory_space=pltpu.SMEM)
VMEM = pl.BlockSpec(memory_space=pltpu.VMEM)
ANY = pl.BlockSpec(memory_space=pl.ANY)


def kernels(tile_shape, modes, width, slots, per_device, groups, cols_along, depth):
    tile_width = tile_shape[-1]
    blocks = tile_width // LANES
    rows = modes * 2 * width // groups
    flops = slots // 2 * modes * 2 * (2 * width) ** 2 * width * 2
    kept_shape = (2 * width + 2 * PACK, modes * width)
    rows_s = pltpu.VMEM((UNROLL, modes * width, 2 * width), jnp.bfloat16)
    columns_s = pltpu.VMEM((UNROLL, 2 * width, modes * width), jnp.bfloat16)
    fields_s = pltpu.VMEM((UNROLL, 2 * width, modes * width), jnp.float32)
    forward = pl.pallas_call(
        lambda *refs: forward_kernel((cols_along, groups, depth, per_device), *refs),
        out_shape=(
            jax.ShapeDtypeStruct((slots + UNROLL, *kept_shape), jnp.bfloat16),
            jax.ShapeDtypeStruct((slots + 2 * UNROLL + 4,), jnp.int32),
        ),
        in_specs=[SMEM, ANY, VMEM, VMEM],
        out_specs=(ANY, SMEM),
        scratch_shapes=[
            pltpu.VMEM((2, blocks, tile_width, LANES), jnp.float32),
            pltpu.VMEM((2, UNROLL, *kept_shape), jnp.bfloat16),
            rows_s,
            pltpu.SemaphoreType.DMA((2 * blocks,)),
            pltpu.SemaphoreType.DMA((2, UNROLL)),
        ],
        compiler_params=pltpu.CompilerParams(vmem_limit_bytes=55 << 20),
        cost_estimate=pl.CostEstimate(flops=flops, bytes_accessed=40_000_000, transcendentals=0),
        name="forward_windows",
    )
    backward = pl.pallas_call(
        lambda *refs: backward_kernel(slots, *refs),
        out_shape=(
            jax.ShapeDtypeStruct(tile_shape, jnp.float32),
            jax.ShapeDtypeStruct((groups, rows + 8, LANES), jnp.float32),
        ),
        in_specs=[SMEM, ANY, VMEM, VMEM, VMEM, VMEM],
        out_specs=(ANY, VMEM),
        scratch_shapes=[
            pltpu.VMEM((2, blocks, tile_width, LANES), jnp.float32),
            pltpu.VMEM((modes, 2, width, LANES), jnp.float32),
            pltpu.VMEM((slots + 1, 1, LANES), jnp.float32),
            pltpu.VMEM((3, UNROLL, *kept_shape), jnp.bfloat16),
            rows_s,
            columns_s,
            fields_s,
            fields_s,
            pltpu.SemaphoreType.DMA((2 * blocks,)),
            pltpu.SemaphoreType.DMA((3, UNROLL)),
        ],
        compiler_params=pltpu.CompilerParams(vmem_limit_bytes=48 << 20),
        cost_estimate=pl.CostEstimate(flops=flops, bytes_accessed=40_000_000, transcendentals=0),
        name="backward_windows",
    )
    return forward, backward


def local(obj, probe, measured, tile_of, inner):
    cols_along = lax.axis_size("ty")
    groups = lax.axis_size("tx") * cols_along
    depth = lax.axis_size("pos")
    modes, _, width, _ = probe.shape
    per_device = measured.shape[0]
    positions = per_device * groups * depth
    slots = groups * CAP
    plane = ("tx", "ty")
    outgoing, own_slots = pl.pallas_call(
        lambda *refs: send_kernel(cols_along, depth, per_device, *refs),
        out_shape=(
            jax.ShapeDtypeStruct((slots, width, width), measured.dtype),
            jax.ShapeDtypeStruct((per_device,), jnp.int32),
        ),
        in_specs=[SMEM, VMEM],
        out_specs=(VMEM, SMEM),
        name="send_slots",
    )(tile_of.reshape(positions), measured)
    arrived = lax.all_to_all(
        outgoing.reshape(groups, CAP, width, width), plane, split_axis=0, concat_axis=0, tiled=True
    ).reshape(slots, width, width)
    packed = (tile_of[:, 0] << TILE_SHIFT) | (inner[:, 0] << ROW_BITS) | inner[:, 1]
    tables = [jnp.asarray(table) for table in dft_blocks(width)]
    rows = modes * 2 * width // groups
    forward, backward = kernels(obj.shape, modes, width, slots, per_device, groups, cols_along, depth)
    kept, listed = forward(packed, obj, probe, tables[1])
    tile_grad, sums = backward(listed, kept, probe, arrived, *tables)
    shares = lax.psum_scatter(tile_grad, "pos", scatter_dimension=1, tiled=True)
    sums = lax.all_to_all(sums, plane, split_axis=0, concat_axis=0, tiled=True)
    probe_part, misfit = pl.pallas_call(
        lambda *refs: receive_kernel(width * width, *refs),
        out_shape=(
            jax.ShapeDtypeStruct((rows, LANES), jnp.float32),
            jax.ShapeDtypeStruct((per_device,), jnp.float32),
        ),
        in_specs=[SMEM, VMEM],
        out_specs=(VMEM, SMEM),
        name="receive_sums",
    )(own_slots, sums)
    hop = 1
    while hop < depth:
        partner = [(z, z ^ hop) for z in range(depth)]
        probe_part = probe_part + lax.ppermute(probe_part, "pos", partner)
        hop *= 2
    probe_total = lax.all_to_all(
        jnp.broadcast_to(probe_part, (groups, rows, LANES)), plane, split_axis=0, concat_axis=0, tiled=True
    )
    return (shares, probe_total.reshape(modes, 2, width, width) * (1.0 / positions), misfit)


def solution(mesh):
    return jax.shard_map(
        local,
        mesh=mesh,
        in_specs=(P(None, "tx", "ty"), P(), P(("tx", "ty", "pos"), None, None), P(), P()),
        out_specs=(P(None, ("tx", "pos"), "ty"), P(), P(("tx", "ty", "pos"))),
        check_vma=False,
    )
```

```python
import jax
import jax.numpy as jnp
import ml_dtypes
import numpy as np
from jax import lax
from jax.experimental import pallas as pl
from jax.experimental.pallas import tpu as pltpu
from jax.sharding import PartitionSpec as P

CAP = 2
UNROLL = 4
STRIP = 16
PACK = 32
LANES = 128
ROW_BITS = 10
TILE_SHIFT = 2 * ROW_BITS
LOW = (1 << ROW_BITS) - 1


def dft_blocks(width):
    counter = np.arange(width, dtype=np.int32)
    product = counter[:, None] * counter[None, :] % width
    angles = product.astype(np.float32) * np.float32(2.0 * np.pi / width)
    factor = np.float32(1.0) / np.sqrt(np.float32(width))
    c = (np.cos(angles) * factor).astype(ml_dtypes.bfloat16)
    s = (-np.sin(angles) * factor).astype(ml_dtypes.bfloat16)
    return np.block([[c, -s], [s, c]]), np.block([[c, s], [-s, c]])


def own_place(cols_along):
    return lax.axis_index("tx") * cols_along + lax.axis_index("ty"), lax.axis_index("pos")


def send_kernel(cols_along, depth, per_device, tile_ref, measured_ref, out_ref, slot_ref, sems):
    tile, plane = own_place(cols_along)
    base = (tile * depth + plane) * per_device
    tiles = [tile_ref[base + i] for i in range(per_device)]
    copies = []
    for i in range(per_device):
        rank = jnp.int32(0)
        for j in range(i):
            rank = rank + (tiles[j] == tiles[i]).astype(jnp.int32)
        slot = tiles[i] * CAP + rank
        slot_ref[i] = slot
        copies.append(pltpu.make_async_copy(measured_ref.at[i], out_ref.at[slot], sems.at[i]))
        copies[-1].start()
    for copy in copies:
        copy.wait()


def list_windows(cols_along, groups, depth, per_device, packed_ref, list_ref):
    tile, plane = own_place(cols_along)

    def one_group(group, count):
        base = (group * depth + plane) * per_device
        values = [packed_ref[base + i] for i in range(per_device)]
        hits = [lax.shift_right_logical(value, TILE_SHIFT) == tile for value in values]
        first = last = jnp.int32(0)
        found = jnp.int32(0)
        for i in range(per_device):
            last = jnp.where(hits[i], values[i], last)
            first = jnp.where(hits[per_device - 1 - i], values[per_device - 1 - i], first)
            found = found + hits[i].astype(jnp.int32)
        for rank, value in enumerate((first, last)):
            list_ref[count + rank] = ((group * CAP + rank) << TILE_SHIFT) | (value & ((1 << TILE_SHIFT) - 1))
        return count + found

    count = lax.fori_loop(0, groups, one_group, jnp.int32(0))
    for u in range(UNROLL):
        list_ref[count + u] = jnp.int32((groups * CAP) << TILE_SHIFT)
    list_ref[groups * CAP + UNROLL] = (count + UNROLL - 1) // UNROLL


def window_of(entry, blocks):
    slot = lax.shift_right_logical(entry, TILE_SHIFT)
    row = lax.shift_right_logical(entry, ROW_BITS) & LOW
    col = entry & LOW
    block = jnp.minimum(lax.shift_right_logical(col, 7), blocks - 2)
    return slot, row, block, col - block * LANES


def patch_spot(width, part, row):
    return pl.ds(2 * width + part * PACK + row % PACK, STRIP), pl.ds(row // PACK * LANES, LANES)


def right_product(field_s, table_ref, half_ref, u):
    width = LANES
    half = jnp.dot(field_s[u], table_ref[...], preferred_element_type=jnp.float32)
    for k in range(field_s.shape[1] // width):
        for h in range(2):
            half_ref[pl.ds(h * width, width), pl.ds(k * width, width)] = half[
                k * width : (k + 1) * width, h * width : (h + 1) * width
            ].astype(jnp.bfloat16)


def forward_kernel(
    sizes,
    packed_ref,
    obj_ref,
    probe_ref,
    y_ref,
    kept_ref,
    list_ref,
    tile_s,
    kept_s,
    field_s,
    sems,
    out_sems,
):
    width = LANES
    modes = probe_ref.shape[0]
    blocks = tile_s.shape[1]
    copies = [
        pltpu.make_async_copy(
            obj_ref.at[a, :, pl.ds(b * LANES, LANES)], tile_s.at[a, b], sems.at[a * blocks + b]
        )
        for a in range(2)
        for b in range(blocks)
    ]
    for copy in copies:
        copy.start()
    list_windows(*sizes, packed_ref, list_ref)
    steps = list_ref[sizes[1] * CAP + UNROLL]
    for copy in copies:
        copy.wait()

    def leaving(n):
        turn = n & 1
        return [
            pltpu.make_async_copy(kept_s.at[turn, u], kept_ref.at[n * UNROLL + u], out_sems.at[turn, u])
            for u in range(UNROLL)
        ]

    lane = lax.broadcasted_iota(jnp.int32, (STRIP, LANES), 1)

    def step(n, carry):
        turn = n & 1

        @pl.when(n >= 2)
        def _():
            for copy in leaving(n - 2):
                copy.wait()

        places = [window_of(list_ref[n * UNROLL + u], blocks) for u in range(UNROLL)]
        for s in range(0, width, STRIP):
            objs = []
            for u in range(UNROLL):
                _, row, block, shift = places[u]
                back_shift = (LANES - shift) & (LANES - 1)
                own = lane < LANES - shift
                parts = []
                for a in range(2):
                    left = pltpu.roll(tile_s[a, block, pl.ds(row + s, STRIP), :], back_shift, 1)
                    right = pltpu.roll(tile_s[a, block + 1, pl.ds(row + s, STRIP), :], back_shift, 1)
                    rounded = jnp.where(own, left, right).astype(jnp.bfloat16)
                    kept_s[(turn, u, *patch_spot(width, a, s))] = rounded
                    parts.append(rounded.astype(jnp.float32))
                objs.append(parts)
            for k in range(modes):
                p_r = probe_ref[k, 0, pl.ds(s, STRIP), :]
                p_i = probe_ref[k, 1, pl.ds(s, STRIP), :]
                for u in range(UNROLL):
                    o_r, o_i = objs[u]
                    at = pl.ds(k * width + s, STRIP)
                    field_s[u, at, pl.ds(0, width)] = (p_r * o_r - p_i * o_i).astype(jnp.bfloat16)
                    field_s[u, at, pl.ds(width, width)] = (p_r * o_i + p_i * o_r).astype(jnp.bfloat16)
        for u in range(UNROLL):
            right_product(field_s, y_ref, kept_s.at[turn, u], u)
        for copy in leaving(n):
            copy.start()
        return carry

    lax.fori_loop(0, steps, step, jnp.int32(0))
    for late in (2, 1):

        @pl.when(steps >= late)
        def _():
            for copy in leaving(steps - late):
                copy.wait()


def backward_kernel(
    slots,
    list_ref,
    kept_ref,
    probe_ref,
    meas_ref,
    x_ref,
    y_ref,
    grad_ref,
    sums_ref,
    acc_s,
    probe_s,
    misfit_s,
    kept_s,
    field_s,
    half_s,
    far_s,
    back_s,
    sems,
    in_sems,
):
    width = LANES
    modes = probe_ref.shape[0]
    blocks = acc_s.shape[1]
    steps = list_ref[slots + UNROLL]

    def coming(n):
        turn = lax.rem(n, 3)
        return [
            pltpu.make_async_copy(kept_ref.at[n * UNROLL + u], kept_s.at[turn, u], in_sems.at[turn, u])
            for u in range(UNROLL)
        ]

    @pl.when(steps > 0)
    def _():
        for copy in coming(0):
            copy.start()

    acc_s[...] = jnp.zeros_like(acc_s)
    probe_s[...] = jnp.zeros_like(probe_s)
    misfit_s[...] = jnp.zeros_like(misfit_s)
    early, late = range(UNROLL // 2), range(UNROLL // 2, UNROLL)
    for u in late:
        back_s[u] = jnp.zeros(back_s.shape[1:], jnp.float32)
        kept_s[2, u, pl.ds(2 * width, 2 * PACK), :] = jnp.zeros((2 * PACK, modes * width), jnp.bfloat16)
    lane = lax.broadcasted_iota(jnp.int32, (STRIP, LANES), 1)

    def far_field(turn, u):
        far_s[u] = jnp.dot(x_ref[...], kept_s[turn, u, pl.ds(0, 2 * width), :], preferred_element_type=jnp.float32)

    def first_product(u, entry):
        slot = lax.shift_right_logical(entry, TILE_SHIFT)
        held = jnp.minimum(slot, slots - 1)
        misfit = jnp.zeros((STRIP, LANES), jnp.float32)
        for s in range(0, width, STRIP):
            fields = [
                far_s[u, pl.ds(h * width + s, STRIP), pl.ds(k * width, width)]
                for k in range(modes)
                for h in range(2)
            ]
            intensity = 1.0 + sum(f * f for f in fields)
            data = meas_ref[held, pl.ds(s, STRIP), :].astype(jnp.float32)
            inverse = lax.rsqrt(intensity)
            gap = intensity * inverse - data
            misfit = misfit + gap * gap
            factor = jnp.where(slot < slots, 1.0 - data * inverse, 0.0)
            for k in range(modes):
                for h in range(2):
                    field_s[u, pl.ds(k * width + s, STRIP), pl.ds(h * width, width)] = (
                        fields[2 * k + h] * factor
                    ).astype(jnp.bfloat16)
        misfit_s[slot] = jnp.sum(misfit, axis=0, keepdims=True)
        right_product(field_s, x_ref, half_s.at[u], u)

    def second_product(u):
        back_s[u] = jnp.dot(y_ref[...], half_s[u], preferred_element_type=jnp.float32)

    def add_strips(turn, members, entries, strips):
        places = [window_of(entry, blocks) for entry in entries]
        count = len(entries)
        for s in strips:
            rows = pl.ds(s, STRIP)
            objs = [
                [kept_s[(turn, u, *patch_spot(width, a, s))].astype(jnp.float32) for a in range(2)] for u in members
            ]
            parts = [None] * count
            for k in range(modes):
                p_r = probe_ref[k, 0, rows, :]
                p_i = probe_ref[k, 1, rows, :]
                sum_r = probe_s[k, 0, rows, :]
                sum_i = probe_s[k, 1, rows, :]
                for n, u in enumerate(members):
                    b_r = back_s[u, rows, pl.ds(k * width, width)]
                    b_i = back_s[u, pl.ds(width + s, STRIP), pl.ds(k * width, width)]
                    o_r, o_i = objs[n]
                    new_r = p_r * b_r + p_i * b_i
                    new_i = p_r * b_i - p_i * b_r
                    parts[n] = [new_r, new_i] if k == 0 else [parts[n][0] + new_r, parts[n][1] + new_i]
                    sum_r = sum_r + (o_r * b_r + o_i * b_i)
                    sum_i = sum_i + (o_r * b_i - o_i * b_r)
                probe_s[k, 0, rows, :] = sum_r
                probe_s[k, 1, rows, :] = sum_i
            for n in range(count):
                _, row, block, shift = places[n]
                keep = lane >= shift
                for a in range(2):
                    turned = pltpu.roll(parts[n][a], shift & (LANES - 1), 1)
                    spot = (a, block, pl.ds(row + s, STRIP), slice(None))
                    acc_s[spot] = acc_s[spot] + jnp.where(keep, turned, 0.0)
                    spot = (a, block + 1, pl.ds(row + s, STRIP), slice(None))
                    acc_s[spot] = acc_s[spot] + jnp.where(keep, 0.0, turned)

    half_way = width // 2
    upper, lower = range(0, half_way, STRIP), range(half_way, width, STRIP)

    def products_beside(turn, members, entries, sums, ahead):
        first_product(members[0], entries[0])
        for u in ahead:
            far_field(turn, u)
        add_strips(*sums, upper)
        for at in range(1, len(members)):
            first_product(members[at], entries[at])
            second_product(members[at - 1])
        add_strips(*sums, lower)
        second_product(members[-1])

    def entries_of(n, members):
        return [list_ref[jnp.maximum(n, 0) * UNROLL + u] for u in members]

    def step(n, carry):
        turn = lax.rem(n, 3)

        @pl.when(n + 1 < steps)
        def _():
            for copy in coming(n + 1):
                copy.start()

        for copy in coming(n):
            copy.wait()
        now = entries_of(n, early)
        for u in early:
            far_field(turn, u)
        products_beside(turn, early, now, (lax.rem(n + 2, 3), late, entries_of(n - 1, late)), late)
        products_beside(turn, late, entries_of(n, late), (turn, early, now), ())
        return carry

    lax.fori_loop(0, steps, step, jnp.int32(0))
    add_strips(lax.rem(steps + 2, 3), late, entries_of(steps - 1, late), range(0, width, STRIP))
    groups = sums_ref.shape[0]
    rows = sums_ref.shape[1] - 8
    copies = [
        pltpu.make_async_copy(
            acc_s.at[a, b], grad_ref.at[a, :, pl.ds(b * LANES, LANES)], sems.at[a * blocks + b]
        )
        for a in range(2)
        for b in range(blocks)
    ]
    for copy in copies:
        copy.start()
    per_plane = width // rows
    for g in range(groups):
        plane, part = divmod(g, per_plane)
        sums_ref[g, pl.ds(0, rows), :] = probe_s[plane // 2, plane % 2, pl.ds(part * rows, rows), :]
        for s in range(CAP):
            sums_ref[g, pl.ds(rows + s, 1), :] = misfit_s[g * CAP + s]
        sums_ref[g, pl.ds(rows + CAP, 8 - CAP), :] = jnp.zeros((8 - CAP, LANES), jnp.float32)
    for copy in copies:
        copy.wait()


def receive_kernel(pixels, slot_ref, sums_ref, probe_ref, misfit_ref):
    groups, rows = sums_ref.shape[0], probe_ref.shape[0]
    total = jnp.zeros((rows, LANES), jnp.float32)
    for g in range(groups):
        total = total + sums_ref[g, pl.ds(0, rows), :]
    probe_ref[...] = total
    for i in range(slot_ref.shape[0]):
        slot = slot_ref[i]
        picked = sums_ref[lax.shift_right_logical(slot, 1), pl.ds(rows + (slot & 1), 1), :]
        misfit_ref[i] = jnp.sum(picked) * (1.0 / pixels)


SMEM = pl.BlockSpec(memory_space=pltpu.SMEM)
VMEM = pl.BlockSpec(memory_space=pltpu.VMEM)
ANY = pl.BlockSpec(memory_space=pl.ANY)


def kernels(tile_shape, modes, width, slots, per_device, groups, cols_along, depth):
    tile_width = tile_shape[-1]
    blocks = tile_width // LANES
    rows = modes * 2 * width // groups
    flops = slots // 2 * modes * 2 * (2 * width) ** 2 * width * 2
    kept_shape = (2 * width + 2 * PACK, modes * width)
    rows_s = pltpu.VMEM((UNROLL, modes * width, 2 * width), jnp.bfloat16)
    columns_s = pltpu.VMEM((UNROLL, 2 * width, modes * width), jnp.bfloat16)
    fields_s = pltpu.VMEM((UNROLL, 2 * width, modes * width), jnp.float32)
    forward = pl.pallas_call(
        lambda *refs: forward_kernel((cols_along, groups, depth, per_device), *refs),
        out_shape=(
            jax.ShapeDtypeStruct((slots + UNROLL, *kept_shape), jnp.bfloat16),
            jax.ShapeDtypeStruct((slots + 2 * UNROLL + 4,), jnp.int32),
        ),
        in_specs=[SMEM, ANY, VMEM, VMEM],
        out_specs=(ANY, SMEM),
        scratch_shapes=[
            pltpu.VMEM((2, blocks, tile_width, LANES), jnp.float32),
            pltpu.VMEM((2, UNROLL, *kept_shape), jnp.bfloat16),
            rows_s,
            pltpu.SemaphoreType.DMA((2 * blocks,)),
            pltpu.SemaphoreType.DMA((2, UNROLL)),
        ],
        compiler_params=pltpu.CompilerParams(vmem_limit_bytes=55 << 20),
        cost_estimate=pl.CostEstimate(flops=flops, bytes_accessed=40_000_000, transcendentals=0),
        name="forward_windows",
    )
    backward = pl.pallas_call(
        lambda *refs: backward_kernel(slots, *refs),
        out_shape=(
            jax.ShapeDtypeStruct(tile_shape, jnp.float32),
            jax.ShapeDtypeStruct((groups, rows + 8, LANES), jnp.float32),
        ),
        in_specs=[SMEM, ANY, VMEM, VMEM, VMEM, VMEM],
        out_specs=(ANY, VMEM),
        scratch_shapes=[
            pltpu.VMEM((2, blocks, tile_width, LANES), jnp.float32),
            pltpu.VMEM((modes, 2, width, LANES), jnp.float32),
            pltpu.VMEM((slots + 1, 1, LANES), jnp.float32),
            pltpu.VMEM((3, UNROLL, *kept_shape), jnp.bfloat16),
            rows_s,
            columns_s,
            fields_s,
            fields_s,
            pltpu.SemaphoreType.DMA((2 * blocks,)),
            pltpu.SemaphoreType.DMA((3, UNROLL)),
        ],
        compiler_params=pltpu.CompilerParams(vmem_limit_bytes=48 << 20),
        cost_estimate=pl.CostEstimate(flops=flops, bytes_accessed=40_000_000, transcendentals=0),
        name="backward_windows",
    )
    return forward, backward


def local(obj, probe, measured, tile_of, inner):
    cols_along = lax.axis_size("ty")
    groups = lax.axis_size("tx") * cols_along
    depth = lax.axis_size("pos")
    modes, _, width, _ = probe.shape
    per_device = measured.shape[0]
    positions = per_device * groups * depth
    slots = groups * CAP
    plane = ("tx", "ty")
    outgoing, own_slots = pl.pallas_call(
        lambda *refs: send_kernel(cols_along, depth, per_device, *refs),
        out_shape=(
            jax.ShapeDtypeStruct((slots, width, width), measured.dtype),
            jax.ShapeDtypeStruct((per_device,), jnp.int32),
        ),
        in_specs=[SMEM, VMEM],
        out_specs=(ANY, SMEM),
        scratch_shapes=[pltpu.SemaphoreType.DMA((per_device,))],
        name="send_slots",
    )(tile_of.reshape(positions), measured)
    arrived = lax.all_to_all(
        outgoing.reshape(groups, CAP, width, width), plane, split_axis=0, concat_axis=0, tiled=True
    ).reshape(slots, width, width)
    packed = (tile_of[:, 0] << TILE_SHIFT) | (inner[:, 0] << ROW_BITS) | inner[:, 1]
    tables = [jnp.asarray(table) for table in dft_blocks(width)]
    rows = modes * 2 * width // groups
    forward, backward = kernels(obj.shape, modes, width, slots, per_device, groups, cols_along, depth)
    kept, listed = forward(packed, obj, probe, tables[1])
    tile_grad, sums = backward(listed, kept, probe, arrived, *tables)
    shares = lax.psum_scatter(tile_grad, "pos", scatter_dimension=1, tiled=True)
    sums = lax.all_to_all(sums, plane, split_axis=0, concat_axis=0, tiled=True)
    probe_part, misfit = pl.pallas_call(
        lambda *refs: receive_kernel(width * width, *refs),
        out_shape=(
            jax.ShapeDtypeStruct((rows, LANES), jnp.float32),
            jax.ShapeDtypeStruct((per_device,), jnp.float32),
        ),
        in_specs=[SMEM, VMEM],
        out_specs=(VMEM, SMEM),
        name="receive_sums",
    )(own_slots, sums)
    hop = 1
    while hop < depth:
        partner = [(z, z ^ hop) for z in range(depth)]
        probe_part = probe_part + lax.ppermute(probe_part, "pos", partner)
        hop *= 2
    probe_total = lax.all_to_all(
        jnp.broadcast_to(probe_part, (groups, rows, LANES)), plane, split_axis=0, concat_axis=0, tiled=True
    )
    return (shares, probe_total.reshape(modes, 2, width, width) * (1.0 / positions), misfit)


def solution(mesh):
    return jax.shard_map(
        local,
        mesh=mesh,
        in_specs=(P(None, "tx", "ty"), P(), P(("tx", "ty", "pos"), None, None), P(), P()),
        out_specs=(P(None, ("tx", "pos"), "ty"), P(), P(("tx", "ty", "pos"))),
        check_vma=False,
    )
```

```python
import jax
import jax.numpy as jnp
import ml_dtypes
import numpy as np
from jax import lax
from jax.experimental import pallas as pl
from jax.experimental.pallas import tpu as pltpu
from jax.sharding import PartitionSpec as P

CAP = 2
UNROLL = 4
STRIP = 16
PACK = 32
LANES = 128
ROW_BITS = 10
TILE_SHIFT = 2 * ROW_BITS
LOW = (1 << ROW_BITS) - 1


def dft_blocks(width):
    counter = np.arange(width, dtype=np.int32)
    product = counter[:, None] * counter[None, :] % width
    angles = product.astype(np.float32) * np.float32(2.0 * np.pi / width)
    factor = np.float32(1.0) / np.sqrt(np.float32(width))
    c = (np.cos(angles) * factor).astype(ml_dtypes.bfloat16)
    s = (-np.sin(angles) * factor).astype(ml_dtypes.bfloat16)
    return np.block([[c, -s], [s, c]]), np.block([[c, s], [-s, c]])


def own_place(cols_along):
    return lax.axis_index("tx") * cols_along + lax.axis_index("ty"), lax.axis_index("pos")


def send_kernel(cols_along, depth, per_device, tile_ref, measured_ref, out_ref, slot_ref):
    tile, plane = own_place(cols_along)
    base = (tile * depth + plane) * per_device
    tiles = [tile_ref[base + i] for i in range(per_device)]
    for i in range(per_device):
        rank = jnp.int32(0)
        for j in range(i):
            rank = rank + (tiles[j] == tiles[i]).astype(jnp.int32)
        slot = tiles[i] * CAP + rank
        slot_ref[i] = slot
        out_ref[slot] = measured_ref[i]


def list_windows(cols_along, groups, depth, per_device, packed_ref, list_ref):
    tile, plane = own_place(cols_along)

    def one_group(group, count):
        base = (group * depth + plane) * per_device
        values = [packed_ref[base + i] for i in range(per_device)]
        hits = [lax.shift_right_logical(value, TILE_SHIFT) == tile for value in values]
        first = last = jnp.int32(0)
        found = jnp.int32(0)
        for i in range(per_device):
            last = jnp.where(hits[i], values[i], last)
            first = jnp.where(hits[per_device - 1 - i], values[per_device - 1 - i], first)
            found = found + hits[i].astype(jnp.int32)
        for rank, value in enumerate((first, last)):
            list_ref[count + rank] = ((group * CAP + rank) << TILE_SHIFT) | (value & ((1 << TILE_SHIFT) - 1))
        return count + found

    count = lax.fori_loop(0, groups, one_group, jnp.int32(0))
    for u in range(UNROLL):
        list_ref[count + u] = jnp.int32((groups * CAP) << TILE_SHIFT)
    list_ref[groups * CAP + UNROLL] = (count + UNROLL - 1) // UNROLL


def window_of(entry, blocks):
    slot = lax.shift_right_logical(entry, TILE_SHIFT)
    row = lax.shift_right_logical(entry, ROW_BITS) & LOW
    col = entry & LOW
    block = jnp.minimum(lax.shift_right_logical(col, 7), blocks - 2)
    return slot, row, block, col - block * LANES


def patch_spot(width, part, row):
    return pl.ds(2 * width + part * PACK + row % PACK, STRIP), pl.ds(row // PACK * LANES, LANES)


def right_product(field_s, table_ref, half_s, u):
    width = LANES
    half = jnp.dot(field_s[u], table_ref[...], preferred_element_type=jnp.float32)
    for k in range(field_s.shape[1] // width):
        for h in range(2):
            half_s[u, pl.ds(h * width, width), pl.ds(k * width, width)] = half[
                k * width : (k + 1) * width, h * width : (h + 1) * width
            ].astype(jnp.bfloat16)


def forward_kernel(
    sizes,
    packed_ref,
    obj_ref,
    probe_ref,
    x_ref,
    y_ref,
    far_ref,
    list_ref,
    tile_s,
    far_s,
    field_s,
    half_s,
    sems,
    out_sems,
):
    width = LANES
    modes = probe_ref.shape[0]
    blocks = tile_s.shape[1]
    copies = [
        pltpu.make_async_copy(
            obj_ref.at[a, :, pl.ds(b * LANES, LANES)], tile_s.at[a, b], sems.at[a * blocks + b]
        )
        for a in range(2)
        for b in range(blocks)
    ]
    for copy in copies:
        copy.start()
    list_windows(*sizes, packed_ref, list_ref)
    steps = list_ref[sizes[1] * CAP + UNROLL]
    for copy in copies:
        copy.wait()

    def leaving(n):
        turn = n & 1
        there = pl.ds(n * UNROLL, UNROLL)
        return (
            pltpu.make_async_copy(far_s.at[turn], far_ref.at[there], out_sems.at[turn]),
        )

    lane = lax.broadcasted_iota(jnp.int32, (STRIP, LANES), 1)

    def step(n, carry):
        turn = n & 1

        @pl.when(n >= 2)
        def _():
            for copy in leaving(n - 2):
                copy.wait()

        places = [window_of(list_ref[n * UNROLL + u], blocks) for u in range(UNROLL)]
        for s in range(0, width, STRIP):
            objs = []
            for u in range(UNROLL):
                _, row, block, shift = places[u]
                back_shift = (LANES - shift) & (LANES - 1)
                own = lane < LANES - shift
                parts = []
                for a in range(2):
                    left = pltpu.roll(tile_s[a, block, pl.ds(row + s, STRIP), :], back_shift, 1)
                    right = pltpu.roll(tile_s[a, block + 1, pl.ds(row + s, STRIP), :], back_shift, 1)
                    rounded = jnp.where(own, left, right).astype(jnp.bfloat16)
                    patch = rounded.astype(jnp.float32)
                    far_s[(turn, u, *patch_spot(width, a, s))] = patch
                    parts.append(patch)
                objs.append(parts)
            for k in range(modes):
                p_r = probe_ref[k, 0, pl.ds(s, STRIP), :]
                p_i = probe_ref[k, 1, pl.ds(s, STRIP), :]
                for u in range(UNROLL):
                    o_r, o_i = objs[u]
                    at = pl.ds(k * width + s, STRIP)
                    field_s[u, at, pl.ds(0, width)] = (p_r * o_r - p_i * o_i).astype(jnp.bfloat16)
                    field_s[u, at, pl.ds(width, width)] = (p_r * o_i + p_i * o_r).astype(jnp.bfloat16)
        for u in range(UNROLL):
            right_product(field_s, y_ref, half_s, u)
        for u in range(UNROLL):
            far_s[turn, u, pl.ds(0, 2 * width), :] = jnp.dot(x_ref[...], half_s[u], preferred_element_type=jnp.float32)
        for copy in leaving(n):
            copy.start()
        return carry

    lax.fori_loop(0, steps, step, jnp.int32(0))
    for late in (2, 1):

        @pl.when(steps >= late)
        def _():
            for copy in leaving(steps - late):
                copy.wait()


def backward_kernel(
    slots,
    list_ref,
    far_ref,
    probe_ref,
    meas_ref,
    x_ref,
    y_ref,
    grad_ref,
    sums_ref,
    acc_s,
    probe_s,
    misfit_s,
    far_s,
    field_s,
    half_s,
    back_s,
    sems,
    in_sems,
):
    width = LANES
    modes = probe_ref.shape[0]
    blocks = acc_s.shape[1]
    steps = list_ref[slots + UNROLL]

    def coming(n):
        turn = n & 1
        there = pl.ds(n * UNROLL, UNROLL)
        return (
            pltpu.make_async_copy(far_ref.at[there], far_s.at[turn], in_sems.at[turn]),
        )

    @pl.when(steps > 0)
    def _():
        for copy in coming(0):
            copy.start()

    acc_s[...] = jnp.zeros_like(acc_s)
    probe_s[...] = jnp.zeros_like(probe_s)
    misfit_s[...] = jnp.zeros_like(misfit_s)
    lane = lax.broadcasted_iota(jnp.int32, (STRIP, LANES), 1)

    def step(n, carry):
        turn = n & 1

        @pl.when(n + 1 < steps)
        def _():
            for copy in coming(n + 1):
                copy.start()

        for copy in coming(n):
            copy.wait()
        entries = [list_ref[n * UNROLL + u] for u in range(UNROLL)]
        for u in range(UNROLL):
            slot = lax.shift_right_logical(entries[u], TILE_SHIFT)
            held = jnp.minimum(slot, slots - 1)
            misfit = jnp.zeros((STRIP, LANES), jnp.float32)
            for s in range(0, width, STRIP):
                fields = [
                    far_s[turn, u, pl.ds(h * width + s, STRIP), pl.ds(k * width, width)]
                    for k in range(modes)
                    for h in range(2)
                ]
                intensity = 1.0 + sum(f * f for f in fields)
                data = meas_ref[held, pl.ds(s, STRIP), :].astype(jnp.float32)
                inverse = lax.rsqrt(intensity)
                gap = intensity * inverse - data
                misfit = misfit + gap * gap
                factor = jnp.where(slot < slots, 1.0 - data * inverse, 0.0)
                for k in range(modes):
                    for h in range(2):
                        field_s[u, pl.ds(k * width + s, STRIP), pl.ds(h * width, width)] = (
                            fields[2 * k + h] * factor
                        ).astype(jnp.bfloat16)
            misfit_s[slot] = jnp.sum(misfit, axis=0, keepdims=True)
            right_product(field_s, x_ref, half_s, u)
            if u:
                back_s[u - 1] = jnp.dot(y_ref[...], half_s[u - 1], preferred_element_type=jnp.float32)
        back_s[UNROLL - 1] = jnp.dot(y_ref[...], half_s[UNROLL - 1], preferred_element_type=jnp.float32)
        places = [window_of(entries[u], blocks) for u in range(UNROLL)]
        for s in range(0, width, STRIP):
            rows = pl.ds(s, STRIP)
            objs = [[far_s[(turn, u, *patch_spot(width, a, s))] for a in range(2)] for u in range(UNROLL)]
            parts = [[None, None] for _ in range(UNROLL)]
            for k in range(modes):
                p_r = probe_ref[k, 0, rows, :]
                p_i = probe_ref[k, 1, rows, :]
                sum_r = probe_s[k, 0, rows, :]
                sum_i = probe_s[k, 1, rows, :]
                for u in range(UNROLL):
                    b_r = back_s[u, rows, pl.ds(k * width, width)]
                    b_i = back_s[u, pl.ds(width + s, STRIP), pl.ds(k * width, width)]
                    o_r, o_i = objs[u]
                    new_r = p_r * b_r + p_i * b_i
                    new_i = p_r * b_i - p_i * b_r
                    parts[u] = [new_r, new_i] if k == 0 else [parts[u][0] + new_r, parts[u][1] + new_i]
                    sum_r = sum_r + (o_r * b_r + o_i * b_i)
                    sum_i = sum_i + (o_r * b_i - o_i * b_r)
                probe_s[k, 0, rows, :] = sum_r
                probe_s[k, 1, rows, :] = sum_i
            for u in range(UNROLL):
                _, row, block, shift = places[u]
                keep = lane >= shift
                for a in range(2):
                    turned = pltpu.roll(parts[u][a], shift & (LANES - 1), 1)
                    spot = (a, block, pl.ds(row + s, STRIP), slice(None))
                    acc_s[spot] = acc_s[spot] + jnp.where(keep, turned, 0.0)
                    spot = (a, block + 1, pl.ds(row + s, STRIP), slice(None))
                    acc_s[spot] = acc_s[spot] + jnp.where(keep, 0.0, turned)
        return carry

    lax.fori_loop(0, steps, step, jnp.int32(0))
    groups = sums_ref.shape[0]
    rows = sums_ref.shape[1] - 8
    copies = [
        pltpu.make_async_copy(
            acc_s.at[a, b], grad_ref.at[a, :, pl.ds(b * LANES, LANES)], sems.at[a * blocks + b]
        )
        for a in range(2)
        for b in range(blocks)
    ]
    for copy in copies:
        copy.start()
    per_plane = width // rows
    for g in range(groups):
        plane, part = divmod(g, per_plane)
        sums_ref[g, pl.ds(0, rows), :] = probe_s[plane // 2, plane % 2, pl.ds(part * rows, rows), :]
        for s in range(CAP):
            sums_ref[g, pl.ds(rows + s, 1), :] = misfit_s[g * CAP + s]
        sums_ref[g, pl.ds(rows + CAP, 8 - CAP), :] = jnp.zeros((8 - CAP, LANES), jnp.float32)
    for copy in copies:
        copy.wait()


def receive_kernel(pixels, slot_ref, sums_ref, probe_ref, misfit_ref):
    groups, rows = sums_ref.shape[0], probe_ref.shape[0]
    total = jnp.zeros((rows, LANES), jnp.float32)
    for g in range(groups):
        total = total + sums_ref[g, pl.ds(0, rows), :]
    probe_ref[...] = total
    for i in range(slot_ref.shape[0]):
        slot = slot_ref[i]
        picked = sums_ref[lax.shift_right_logical(slot, 1), pl.ds(rows + (slot & 1), 1), :]
        misfit_ref[i] = jnp.sum(picked) * (1.0 / pixels)


SMEM = pl.BlockSpec(memory_space=pltpu.SMEM)
VMEM = pl.BlockSpec(memory_space=pltpu.VMEM)
ANY = pl.BlockSpec(memory_space=pl.ANY)


def kernels(tile_shape, modes, width, slots, per_device, groups, cols_along, depth):
    tile_width = tile_shape[-1]
    blocks = tile_width // LANES
    rows = modes * 2 * width // groups
    flops = slots // 2 * modes * 2 * (2 * width) ** 2 * width * 2
    far_buffers = [
        pltpu.VMEM((turns, UNROLL, 2 * width + 2 * PACK, modes * width), jnp.float32) for turns in (2, 3)
    ]
    staging = [
        pltpu.VMEM((UNROLL, modes * width, 2 * width), jnp.bfloat16),
        pltpu.VMEM((UNROLL, 2 * width, modes * width), jnp.bfloat16),
    ]
    forward = pl.pallas_call(
        lambda *refs: forward_kernel((cols_along, groups, depth, per_device), *refs),
        out_shape=(
            jax.ShapeDtypeStruct((slots + UNROLL, 2 * width + 2 * PACK, modes * width), jnp.float32),
            jax.ShapeDtypeStruct((slots + 2 * UNROLL + 4,), jnp.int32),
        ),
        in_specs=[SMEM, ANY, VMEM, VMEM, VMEM],
        out_specs=(ANY, SMEM),
        scratch_shapes=[
            pltpu.VMEM((2, blocks, tile_width, LANES), jnp.float32),
            far_buffers[0],
            *staging,
            pltpu.SemaphoreType.DMA((2 * blocks,)),
            pltpu.SemaphoreType.DMA((2,)),
        ],
        compiler_params=pltpu.CompilerParams(vmem_limit_bytes=55 << 20),
        cost_estimate=pl.CostEstimate(flops=flops, bytes_accessed=40_000_000, transcendentals=0),
        name="forward_windows",
    )
    backward = pl.pallas_call(
        lambda *refs: backward_kernel(slots, *refs),
        out_shape=(
            jax.ShapeDtypeStruct(tile_shape, jnp.float32),
            jax.ShapeDtypeStruct((groups, rows + 8, LANES), jnp.float32),
        ),
        in_specs=[SMEM, ANY, VMEM, VMEM, VMEM, VMEM],
        out_specs=(ANY, VMEM),
        scratch_shapes=[
            pltpu.VMEM((2, blocks, tile_width, LANES), jnp.float32),
            pltpu.VMEM((modes, 2, width, LANES), jnp.float32),
            pltpu.VMEM((slots + 1, 1, LANES), jnp.float32),
            far_buffers[1],
            *staging,
            pltpu.VMEM((UNROLL, 2 * width, modes * width), jnp.float32),
            pltpu.SemaphoreType.DMA((2 * blocks,)),
            pltpu.SemaphoreType.DMA((3,)),
        ],
        compiler_params=pltpu.CompilerParams(vmem_limit_bytes=48 << 20),
        cost_estimate=pl.CostEstimate(flops=flops, bytes_accessed=40_000_000, transcendentals=0),
        name="backward_windows",
    )
    return forward, backward


def local(obj, probe, measured, tile_of, inner):
    cols_along = lax.axis_size("ty")
    groups = lax.axis_size("tx") * cols_along
    depth = lax.axis_size("pos")
    modes, _, width, _ = probe.shape
    per_device = measured.shape[0]
    positions = per_device * groups * depth
    slots = groups * CAP
    plane = ("tx", "ty")
    outgoing, own_slots = pl.pallas_call(
        lambda *refs: send_kernel(cols_along, depth, per_device, *refs),
        out_shape=(
            jax.ShapeDtypeStruct((slots, width, width), measured.dtype),
            jax.ShapeDtypeStruct((per_device,), jnp.int32),
        ),
        in_specs=[SMEM, VMEM],
        out_specs=(VMEM, SMEM),
        name="send_slots",
    )(tile_of.reshape(positions), measured)
    arrived = lax.all_to_all(
        outgoing.reshape(groups, CAP, width, width), plane, split_axis=0, concat_axis=0, tiled=True
    ).reshape(slots, width, width)
    packed = (tile_of[:, 0] << TILE_SHIFT) | (inner[:, 0] << ROW_BITS) | inner[:, 1]
    tables = [jnp.asarray(table) for table in dft_blocks(width)]
    rows = modes * 2 * width // groups
    forward, backward = kernels(obj.shape, modes, width, slots, per_device, groups, cols_along, depth)
    far, listed = forward(packed, obj, probe, *tables)
    tile_grad, sums = backward(listed, far, probe, arrived, *tables)
    shares = lax.psum_scatter(tile_grad, "pos", scatter_dimension=1, tiled=True)
    sums = lax.all_to_all(sums, plane, split_axis=0, concat_axis=0, tiled=True)
    probe_part, misfit = pl.pallas_call(
        lambda *refs: receive_kernel(width * width, *refs),
        out_shape=(
            jax.ShapeDtypeStruct((rows, LANES), jnp.float32),
            jax.ShapeDtypeStruct((per_device,), jnp.float32),
        ),
        in_specs=[SMEM, VMEM],
        out_specs=(VMEM, SMEM),
        name="receive_sums",
    )(own_slots, sums)
    hop = 1
    while hop < depth:
        partner = [(z, z ^ hop) for z in range(depth)]
        probe_part = probe_part + lax.ppermute(probe_part, "pos", partner)
        hop *= 2
    probe_total = lax.all_to_all(
        jnp.broadcast_to(probe_part, (groups, rows, LANES)), plane, split_axis=0, concat_axis=0, tiled=True
    )
    return (shares, probe_total.reshape(modes, 2, width, width) * (1.0 / positions), misfit)


def solution(mesh):
    return jax.shard_map(
        local,
        mesh=mesh,
        in_specs=(P(None, "tx", "ty"), P(), P(("tx", "ty", "pos"), None, None), P(), P()),
        out_specs=(P(None, ("tx", "pos"), "ty"), P(), P(("tx", "ty", "pos"))),
        check_vma=False,
    )
```
